512 devices in a mesh: flux: 16 (over z), obs: 32 (over y, x, core).
Axes of the slice: x: 4, y: 4, z: 16, core: 2. Of those that a mesh axis runs over, the one named last changes fastest.
Arguments:
- footprint: bfloat16 [4096, 4, 4, 2, 4096], P(('flux', 'obs')), may hold values from 0.00049972534 to 0.049804688
- obs_hour: int32 [4096, 4], P(('flux', 'obs')), may hold values from 0 to 3
- tile_list: int32 [4096, 4], P(('flux', 'obs')), may hold values from 0 to 511, as said below
- tile_row: int32 [512], replicated, may hold values from 0 to 511, as said below
- flux: bfloat16 [512, 5, 4096], P('flux'), may hold values from -6 to 6
- observed: float32 [4096, 4], P(('flux', 'obs')), may hold values from -18 to 18
- obs_var: float32 [4096, 4], P(('flux', 'obs')), may hold values from 0.5 to 4
Outputs:
- modeled: float32 [4096, 4], P(('flux', 'obs'))
- gradient: float32 [512, 5, 4096], P('flux', None, 'obs')
The draws below stay inside these ranges and needn't reach their ends.
Inputs may be any that keep to these rules, and one draw needn't show every extreme that they name: `tile_row`: A permutation: every tile has its own storage row, and the row r lies on index r // 32 of flux. `tile_list`: among the 32 listed tiles of one device's 8 blocks, at most 4 have storage rows on one index of flux; on every device some index of flux gets exactly 4.
All inputs are finite; a program needn't handle non-finite values.
Results may differ from the reference program's by a relative error of at most 0.0019.
Values may be sent and summed in bfloat16 or wider, within the bound.
A program may use at most 64 MiB of HBM per device.

```python
import math
import jax
import jax.numpy as jnp
from jax import lax

TILE_CELLS = 4096
LAGS = 2
SPAN_HOURS = 4
OBS_BLK = 4
KSLOT = 4
NTILES = 512
BLK_DEV = 8
HOURS = 5
TILE_DEV = 32
BLOCKS = 4096
CAP = 4


def storage_order(key):
    return jax.random.permutation(jax.random.fold_in(key, 11), NTILES).astype(jnp.int32)


def draw_tile_row(key, part):
    return storage_order(key)


def draw_tile_list(key, part):
    storage = storage_order(key)
    inverse = jnp.argsort(storage, stable=True).astype(jnp.int32)
    owners = NTILES // TILE_DEV
    devices = BLOCKS // BLK_DEV
    columns = devices // owners
    slot_count = BLK_DEV * KSLOT
    owner_pool = jnp.arange(owners * CAP, dtype=jnp.int32) // CAP

    def one_device(device):
        column = device % columns
        hot_key = jax.random.fold_in(jax.random.fold_in(key, 29), column)
        hottest = jax.random.randint(hot_key, (), 0, owners)
        device_key = jax.random.fold_in(jax.random.fold_in(key, 37), device)
        first_key, second_key, third_key = jax.random.split(device_key, 3)
        ranking = jax.random.permutation(first_key, owners * CAP).astype(jnp.int32)
        scores = jnp.where(owner_pool == hottest, ranking - owners * CAP, ranking)
        chosen = owner_pool[jnp.argsort(scores, stable=True)][:slot_count]
        chosen = chosen[jax.random.permutation(second_key, slot_count)]
        samples = jax.random.randint(third_key, (3, slot_count), 0, TILE_DEV)
        local_index = jnp.min(samples, axis=0)
        return inverse[chosen * TILE_DEV + local_index].reshape(BLK_DEV, KSLOT)
    listed = jax.vmap(one_device)(jnp.arange(devices, dtype=jnp.int32))
    return listed.reshape(BLOCKS, KSLOT).astype(jnp.int32)


def place_ends(drawn, own_key, low, top_value):
    index_at = [jax.random.randint(jax.random.fold_in(own_key, axis), (), 0, length) for axis, length in enumerate(drawn.shape)]
    widest = drawn.shape.index(max(drawn.shape))
    beside = index_at[:widest] + [(index_at[widest] + 1) % drawn.shape[widest]] + index_at[widest + 1:]
    return drawn.at[tuple(index_at)].set(low).at[tuple(beside)].set(top_value)


def block_levels(own_key, extent, cuts, least, largest):
    factor_of = 1.0
    for dim, shards_of in cuts:
        heights = jax.random.uniform(jax.random.fold_in(jax.random.fold_in(own_key, 6), dim), (shards_of,), jnp.float32, least / len(cuts), largest / len(cuts))
        factor_of = factor_of * jnp.repeat(jnp.exp(heights), extent[dim] // shards_of).reshape((-1,) + (1,) * (len(extent) - 1 - dim))
    return factor_of


def bell_draw(stream_key, dims, scale, limit, cuts=(), kind=jnp.bfloat16):
    values = jax.random.normal(stream_key, dims, jnp.float32) * scale
    if len(cuts) > 0:
        values = block_levels(stream_key, dims, cuts, -0.22, 0.18) * values
    return jnp.clip(values, min=-limit, max=limit).astype(kind)


def setup_inputs(seed: int = 0) -> dict:
    streams_of = jax.random.split(jax.random.key(seed), 8)
    return {
        "footprint": jnp.clip(jnp.exp(math.log(0.049804688) - 4.6018058 * jax.random.uniform(streams_of[0], (BLOCKS, KSLOT, OBS_BLK, LAGS, TILE_CELLS), jnp.float32) ** block_levels(streams_of[0], (BLOCKS, KSLOT, OBS_BLK, LAGS, TILE_CELLS), ((0, 512),), -0.2, 0.2)), 0.00049972534, 0.049804688).astype(jnp.bfloat16),
        "obs_hour": place_ends(jax.random.randint(streams_of[1], (BLOCKS, OBS_BLK), 0, SPAN_HOURS), jax.random.fold_in(streams_of[1], 1), 0, SPAN_HOURS - 1).astype(jnp.int32),
        "tile_list": draw_tile_list(jax.random.fold_in(streams_of[7], 71), 0),
        "tile_row": draw_tile_row(jax.random.fold_in(streams_of[7], 71), 0),
        "flux": bell_draw(streams_of[4], (NTILES, HOURS, TILE_CELLS), 1.0, 6.0, ((0, 16),)),
        "observed": bell_draw(streams_of[5], (BLOCKS, OBS_BLK), 3.0, 18.0, ((0, 512),), jnp.float32),
        "obs_var": jnp.clip(jnp.exp(math.log(4.0) - 2.0794415 * jax.random.uniform(streams_of[6], (BLOCKS, OBS_BLK), jnp.float32) ** block_levels(streams_of[6], (BLOCKS, OBS_BLK), ((0, 512),), -0.2, 0.2)), 0.5, 4.0),
    }


def hour_select(hour_rows):
    target = hour_rows[:, :, None] + jnp.arange(LAGS, dtype=jnp.int32)[None, None, :]
    return (target[..., None] == jnp.arange(HOURS, dtype=jnp.int32)).astype(jnp.float32)


def reference(footprint, obs_hour, tile_list, tile_row, flux, observed, obs_var):
    groups = BLOCKS // BLK_DEV
    storage = tile_row[tile_list].astype(jnp.int32)
    foot_groups = footprint.reshape(groups, BLK_DEV, KSLOT, OBS_BLK, LAGS, TILE_CELLS)
    hour_groups = obs_hour.reshape(groups, BLK_DEV, OBS_BLK)
    row_groups = storage.reshape(groups, BLK_DEV, KSLOT)

    def forward(pieces):
        footprints, hour_rows, rows_here = pieces
        windows = flux[rows_here].astype(jnp.float32)
        select = hour_select(hour_rows)
        products = jnp.einsum("bkolc,bkhc->bkolh", footprints.astype(jnp.float32), windows, precision=lax.Precision.HIGHEST)
        partial_value = jnp.sum(products * select[:, None], axis=(3, 4))
        return jnp.sum(partial_value, axis=1)

    modeled = lax.map(forward, (foot_groups, hour_groups, row_groups)).reshape(BLOCKS, OBS_BLK)
    scaled = ((modeled - observed) / obs_var).astype(jnp.bfloat16)
    scaled_groups = scaled.reshape(groups, BLK_DEV, OBS_BLK)

    def adjoint(running, pieces):
        footprints, hour_rows, rows_here, scaled_here = pieces
        coefficient = (hour_select(hour_rows) * scaled_here.astype(jnp.float32)[:, :, None, None]).astype(jnp.bfloat16)
        contributions = jnp.einsum("bolh,bkolc->bkhc", coefficient.astype(jnp.float32), footprints.astype(jnp.float32), precision=lax.Precision.HIGHEST)
        updated = running.at[rows_here.reshape(-1)].add(contributions.reshape(BLK_DEV * KSLOT, HOURS, TILE_CELLS))
        return updated, jnp.zeros((), jnp.float32)

    start = jnp.zeros((NTILES, HOURS, TILE_CELLS), jnp.float32)
    gradient = lax.scan(adjoint, start, (foot_groups, hour_groups, row_groups, scaled_groups))[0]
    return modeled, gradient
```

```python
import jax
import jax.numpy as jnp
from jax import lax
from jax.sharding import PartitionSpec as P


def shards(footprint, obs_hour, tile_list, tile_row, flux, observed, obs_var):
    columns = lax.axis_size("obs")
    block_count, slot_width, sounding_count, lag_count, cell_count = footprint.shape
    tile_count, hour_count, _ = flux.shape
    chunk = cell_count // columns
    me = lax.axis_index("obs")
    table_hits = tile_list[..., None] == jnp.arange(tile_row.shape[0], dtype=jnp.int32)
    storage = jnp.sum(jnp.where(table_hits, tile_row, 0), axis=-1)
    numbers = jnp.concatenate(
        [storage.astype(jnp.float32), obs_hour.astype(jnp.float32), observed, obs_var], axis=1
    )
    numbers = lax.all_gather(numbers, "obs", axis=0, tiled=True)
    rows = numbers[:, 0:4].astype(jnp.int32)
    hours = numbers[:, 4:8].astype(jnp.int32)
    own_flux = lax.dynamic_slice_in_dim(flux, me * chunk, chunk, axis=2)
    all_flux = lax.all_gather(own_flux, "flux", axis=0, tiled=True)
    total = all_flux.shape[0]
    feet = footprint.reshape(-1, columns, chunk).transpose(1, 0, 2)
    feet = lax.all_to_all(feet, "obs", split_axis=0, concat_axis=0, tiled=True)
    blocks = block_count * columns
    feet = feet.reshape(blocks, slot_width, sounding_count, lag_count, chunk)
    onehot = rows.reshape(-1)[:, None] == jnp.arange(total, dtype=jnp.int32)[None, :]
    windows = jnp.dot(
        onehot.astype(jnp.bfloat16),
        all_flux.reshape(total, hour_count * chunk),
        preferred_element_type=jnp.float32,
    ).reshape(blocks, slot_width, hour_count, chunk)
    hour_at = hours[:, :, None] + jnp.arange(lag_count, dtype=jnp.int32)
    select = hour_at[..., None] == jnp.arange(hour_count, dtype=jnp.int32)
    picked = 0.0
    for h in range(hour_count):
        picked = picked + jnp.where(
            select[:, None, :, :, h, None], windows[:, :, None, None, h, :], 0.0
        )
    partial_value = jnp.sum(feet.astype(jnp.float32) * picked, axis=(1, 3, 4))
    modeled_all = lax.psum(partial_value, "obs")
    scaled = ((modeled_all - numbers[:, 8:12]) / numbers[:, 12:16]).astype(jnp.bfloat16)
    modeled = lax.dynamic_slice_in_dim(modeled_all, me * block_count, block_count, axis=0)
    coefficient = jnp.where(select, scaled.astype(jnp.float32)[:, :, None, None], 0.0)
    terms = []
    for h in range(hour_count):
        terms.append(
            jnp.sum(feet.astype(jnp.float32) * coefficient[:, None, :, :, h, None], axis=(2, 3))
        )
    terms = jnp.stack(terms, axis=2).reshape(blocks * slot_width, hour_count * chunk)
    high = terms.astype(jnp.bfloat16)
    low = (terms - high.astype(jnp.float32)).astype(jnp.bfloat16)
    spread = onehot.astype(jnp.bfloat16)
    summed = lax.dot_general(
        spread, high, (((0,), (0,)), ((), ())), preferred_element_type=jnp.float32
    ) + lax.dot_general(spread, low, (((0,), (0,)), ((), ())), preferred_element_type=jnp.float32)
    gradient = lax.psum_scatter(
        summed.reshape(total, hour_count, chunk), "flux", scatter_dimension=0, tiled=True
    )
    return modeled, gradient


def solution(mesh):
    placed = (
        P(("flux", "obs"), None, None, None, None),
        P(("flux", "obs"), None),
        P(("flux", "obs"), None),
        P(),
        P("flux", None, None),
        P(("flux", "obs"), None),
        P(("flux", "obs"), None),
    )
    return jax.shard_map(
        shards,
        mesh=mesh,
        in_specs=placed,
        out_specs=(P(("flux", "obs"), None), P("flux", None, "obs")),
        check_vma=False,
    )
```

```python
import functools

import jax
import jax.numpy as jnp
from jax import lax
from jax.experimental import pallas as pl
from jax.experimental.pallas import tpu as pltpu
from jax.sharding import PartitionSpec as P

MESH = pl.DeviceIdType.MESH
LANES = 128
ROW = 4


def kernel(
    nz, nobs, hours, feet, flux, meta, mod, grad,
    held, window, metas, pairs, onehot, spread, near, parts, total, high, low, mine, down, up,
    local_sem, ring_send, ring_recv, meta_send, meta_recv, feet_send, feet_recv,
    part_send, part_recv, down_send, down_recv, up_send, up_recv,
):
    f32, bf16 = jnp.float32, jnp.bfloat16
    chips = nobs // 2
    tiles = flux.shape[1]
    blocks = 8
    width = 2 * blocks
    slots = chips * width
    z = lax.axis_index("flux")
    me = lax.axis_index("obs")
    chip, core = me // 2, lax.rem(me, 2)
    y, x = chip // ROW, lax.rem(chip, ROW)
    above, below = lax.rem(z + 1, nz), lax.rem(z + nz - 1, nz)
    plus = nz // 2
    minus = nz - 1 - plus

    def target(t):
        c = t // 2
        there = lax.rem(y + c // ROW, chips // ROW) * ROW + lax.rem(x + lax.rem(c, ROW), ROW)
        return there * 2 + lax.rem(core + t, 2)

    def source_chip(c):
        return lax.rem(y + chips // ROW - c // ROW, chips // ROW) * ROW + lax.rem(
            x + ROW - lax.rem(c, ROW), ROW
        )

    def source(t):
        return source_chip(t // 2) * 2 + lax.rem(core + t, 2)

    def place(i):
        return held.at[i // 2, :, pl.ds(lax.rem(i, 2) * 64, 64), :]

    def remote(src, dst, send, recv, to):
        return pltpu.make_async_remote_copy(
            src_ref=src, dst_ref=dst, send_sem=send, recv_sem=recv,
            device_id=to, device_id_type=MESH,
        )

    def feet_copy(t):
        to = target(t)
        return remote(feet.at[to], place(me), feet_send.at[t], feet_recv.at[t], (z, to))

    def feet_arrival(t):
        return remote(feet.at[me], place(source(t)), feet_send.at[t], feet_recv.at[t], (z, target(t)))

    def meta_copy(t, i):
        return remote(meta, metas.at[i], meta_send.at[t], meta_recv.at[t], (z, target(t)))

    def part_copy(t, i):
        return remote(parts.at[me], parts.at[i], part_send.at[t], part_recv.at[t], (z, target(t)))

    def ring_copy(way, s, origin):
        at = window.at[:, pl.ds(lax.rem(origin + nz, nz) * tiles, tiles), :]
        return remote(at, at, ring_send.at[way, s], ring_recv.at[way, s], (above if way == 0 else below, me))

    own_feet = pltpu.make_async_copy(feet.at[me], place(me), local_sem.at[0])
    own_flux = pltpu.make_async_copy(
        flux.at[:, :, pl.ds(me * LANES, LANES)],
        window.at[:, pl.ds(z * tiles, tiles), :],
        local_sem.at[1],
    )
    own_feet.start()
    own_flux.start()
    metas[me] = meta[...]

    barrier = pltpu.get_barrier_semaphore()

    @pl.loop(1, nobs)
    def _(t):
        pl.semaphore_signal(barrier, inc=1, device_id=(z, target(t)), device_id_type=MESH)

    pl.semaphore_signal(barrier, inc=1, device_id=(above, me), device_id_type=MESH)
    pl.semaphore_signal(barrier, inc=1, device_id=(below, me), device_id_type=MESH)
    own_flux.wait()
    pl.semaphore_wait(barrier, nobs + 1)

    ring_copy(0, 0, z).start()
    if minus > 0:
        ring_copy(1, 0, z).start()

    @pl.loop(1, nobs)
    def _(t):
        meta_copy(t, me).start()
        feet_copy(t).start()

    for s in range(1, plus):
        ring_copy(0, s - 1, z - s).wait_recv()
        ring_copy(0, s, z - s).start()
        if s < minus:
            ring_copy(1, s - 1, z + s).wait_recv()
            ring_copy(1, s, z + s).start()
    ring_copy(0, plus - 1, z - plus).wait_recv()
    if minus > 0:
        ring_copy(1, minus - 1, z + minus).wait_recv()

    @pl.loop(1, nobs)
    def _(t):
        meta_copy(t, source(t)).wait_recv()

    lane = lax.broadcasted_iota(jnp.int32, (8, LANES), 1)
    per_half = nobs // 2
    halves = []
    for half in range(2):
        gathered = jnp.zeros((8, LANES), f32)
        for i in range(per_half):
            gathered = jnp.where(lane // blocks == i, metas[half * per_half + i], gathered)
        halves.append(gathered)

    @pl.loop(0, chips)
    def _(g):
        pairs[g] = jnp.where(lane < 64, metas[2 * g], metas[2 * g + 1])

    count = nz * tiles
    for half in range(2):
        upright = halves[half].T
        for k in range(4):
            at = k * slots + half * LANES
            across = halves[half][4 + k : 5 + k, :]
            tile_at = lax.broadcasted_iota(jnp.int32, (count, LANES), 0).astype(f32)
            spread[:, at : at + LANES] = jnp.where(tile_at == across, 1.0, 0.0).astype(bf16)
            along = upright[:, 4 + k : 5 + k]
            tile_on = lax.broadcasted_iota(jnp.int32, (LANES, count), 1).astype(f32)
            onehot[at : at + LANES, :] = jnp.where(tile_on == along, 1.0, 0.0).astype(bf16)

    @pl.loop(0, 4)
    def _(k):
        begin = pl.multiple_of(k * slots, LANES)
        pick = onehot[pl.ds(begin, slots), :]
        for h in range(hours):
            near[h, pl.ds(begin, slots), :] = jnp.dot(
                pick, window[h], preferred_element_type=f32
            ).astype(bf16)

    mask_row = lax.broadcasted_iota(jnp.int32, (hours * width, LANES), 0)
    mask_lane = lax.broadcasted_iota(jnp.int32, (hours * width, LANES), 1)
    same_block = lax.rem(mask_row, width) == mask_lane // 8
    hour_of = (mask_row // width).astype(f32)

    def mask(g):
        return same_block & (hour_of == pairs[g, 0:1, :])

    def group_feet(g):
        return jnp.concatenate([held[g, k] for k in range(4)], axis=1)

    own_feet.wait()

    @pl.loop(0, chips)
    def _(c):
        @pl.when(c > 0)
        def _():
            feet_arrival(2 * c).wait_recv()

        feet_arrival(2 * c + 1).wait_recv()
        g = source_chip(c)
        flux_rows = []
        for k in range(4):
            begin = pl.multiple_of(k * slots + g * width, width)
            flux_rows.append(
                jnp.concatenate([near[h, pl.ds(begin, width), :] for h in range(hours)], axis=0)
            )
        products = lax.dot_general(
            jnp.concatenate(flux_rows, axis=1), group_feet(g),
            (((1,), (1,)), ((), ())), preferred_element_type=f32,
        )
        parts[me, pl.ds(g, 1), :] = jnp.sum(
            jnp.where(mask(g), products, 0.0), axis=0, keepdims=True
        )

    @pl.loop(1, nobs)
    def _(t):
        part_copy(t, me).start()

    @pl.loop(1, nobs)
    def _(t):
        part_copy(t, source(t)).wait_recv()

    summed = parts[0]
    for i in range(1, nobs):
        summed = summed + parts[i]
    even = lax.rem(lax.broadcasted_iota(jnp.int32, (chips, LANES), 1), 2) == 0
    total[...] = summed + jnp.where(
        even, pltpu.roll(summed, LANES - 1, 1), pltpu.roll(summed, 1, 1)
    )
    mod[...] = jnp.broadcast_to(total[pl.ds(chip, 1), :], mod.shape)

    @pl.loop(0, chips)
    def _(g):
        misfit = (total[pl.ds(g, 1), :] - pairs[g, 1:2, :]) / pairs[g, 2:3, :]
        scaled = misfit.astype(bf16).astype(f32)
        coefficient = jnp.where(mask(g), scaled, 0.0).astype(bf16)
        terms = jnp.dot(coefficient, group_feet(g), preferred_element_type=f32)
        upper = terms.astype(bf16)
        lower = (terms - upper.astype(f32)).astype(bf16)
        for k in range(4):
            begin = pl.multiple_of(k * slots + g * width, width)
            for h in range(hours):
                cut = (slice(h * width, (h + 1) * width), slice(k * LANES, (k + 1) * LANES))
                high[pl.ds(begin, width), h * LANES : (h + 1) * LANES] = upper[cut]
                low[pl.ds(begin, width), h * LANES : (h + 1) * LANES] = lower[cut]

    @pl.loop(0, count // LANES)
    def _(q):
        pick = spread[pl.ds(pl.multiple_of(q * LANES, LANES), LANES), :]
        rows = jnp.dot(pick, high[...], preferred_element_type=f32) + jnp.dot(
            pick, low[...], preferred_element_type=f32
        )
        for i in range(LANES // tiles):
            for h in range(hours):
                mine[q * (LANES // tiles) + i, h] = rows[
                    i * tiles : (i + 1) * tiles, h * LANES : (h + 1) * LANES
                ]

    def down_copy(s, p):
        at = lax.rem(z + nz - plus + s, nz)
        if isinstance(s, int) and s == 0:
            src = mine.at[at, p]
        else:
            src = down.at[s - 1, p]
        return remote(src, down.at[s, p], down_send.at[s, p], down_recv.at[s, p], (below, me))

    def up_copy(s, p):
        at = lax.rem(z + minus - s + nz, nz)
        if isinstance(s, int) and s == 0:
            src = mine.at[at, p]
        else:
            src = up.at[s - 1, p]
        return remote(src, up.at[s, p], up_send.at[s, p], up_recv.at[s, p], (above, me))

    def down_step(s, p):
        down_copy(s - 1 if not isinstance(s, int) else max(s - 1, 0), p).wait_recv()
        down[s - 1, p] += mine[lax.rem(z + nz - plus + s, nz), p]
        down_copy(s, p).start()

    def up_step(s, p):
        up_copy(s - 1 if not isinstance(s, int) else max(s - 1, 0), p).wait_recv()
        up[s - 1, p] += mine[lax.rem(z + minus - s + nz, nz), p]
        up_copy(s, p).start()

    for p in range(hours):
        down_copy(0, p).start()
        if minus > 0:
            up_copy(0, p).start()
    for s in range(1, plus):
        for p in range(hours):
            down_step(s, p)
            if s < minus:
                up_step(s, p)
    for p in range(hours):
        down_copy(plus - 1, p).wait_recv()
        value = mine[z, p] + down[plus - 1, p]
        if minus > 0:
            up_copy(minus - 1, p).wait_recv()
            value = value + up[minus - 1, p]
        grad[p] = value

    for s in range(plus):
        ring_copy(0, s, z).wait_send()
        for p in range(hours):
            down_copy(s, p).wait_send()
    for s in range(minus):
        ring_copy(1, s, z).wait_send()
        for p in range(hours):
            up_copy(s, p).wait_send()

    @pl.loop(1, nobs)
    def _(t):
        meta_copy(t, me).wait_send()
        feet_copy(t).wait_send()
        part_copy(t, me).wait_send()


def shards(footprint, obs_hour, tile_list, tile_row, flux, observed, obs_var):
    nobs, nz = lax.axis_size("obs"), lax.axis_size("flux")
    block_count, slot_width, sounding_count, lag_count, cell_count = footprint.shape
    tile_count, hour_count, _ = flux.shape
    me = lax.axis_index("obs")
    f32, bf16 = jnp.float32, jnp.bfloat16
    table_hits = tile_list[..., None] == jnp.arange(tile_row.shape[0], dtype=jnp.int32)
    storage = jnp.sum(jnp.where(table_hits, tile_row, 0), axis=-1).astype(f32)

    def wide(values):
        return jnp.tile(jnp.repeat(values.reshape(1, -1), lag_count, axis=1), (1, 2))

    lags = (jnp.arange(LANES) % lag_count).astype(f32)[None]
    meta = jnp.concatenate(
        [
            wide(obs_hour.astype(f32)) + lags,
            wide(observed),
            wide(obs_var),
            jnp.zeros((1, LANES), f32),
            jnp.tile(storage.T, (1, LANES // block_count)),
        ],
        axis=0,
    )
    feet = footprint.reshape(
        block_count, slot_width, sounding_count * lag_count, nobs, LANES
    ).transpose(3, 1, 0, 2, 4).reshape(nobs, slot_width, 64, LANES)
    chips, count, slots = nobs // 2, nz * tile_count, nobs * block_count
    plus = nz // 2
    minus = max(nz - 1 - plus, 1)
    dma = pltpu.SemaphoreType.DMA
    mod, grad = pl.pallas_call(
        functools.partial(kernel, nz, nobs, hour_count),
        out_shape=(
            jax.ShapeDtypeStruct((8, LANES), f32),
            jax.ShapeDtypeStruct((hour_count, tile_count, LANES), f32),
        ),
        in_specs=[
            pl.BlockSpec(memory_space=pl.ANY),
            pl.BlockSpec(memory_space=pl.ANY),
            pl.BlockSpec(memory_space=pltpu.VMEM),
        ],
        out_specs=(pl.BlockSpec(memory_space=pltpu.VMEM),) * 2,
        scratch_shapes=[
            pltpu.VMEM((chips, slot_width, LANES, LANES), bf16),
            pltpu.VMEM((hour_count, count, LANES), bf16),
            pltpu.VMEM((nobs, 8, LANES), f32),
            pltpu.VMEM((chips, 8, LANES), f32),
            pltpu.VMEM((slots * slot_width, count), bf16),
            pltpu.VMEM((count, slots * slot_width), bf16),
            pltpu.VMEM((hour_count, slots * slot_width, LANES), bf16),
            pltpu.VMEM((nobs, chips, LANES), f32),
            pltpu.VMEM((chips, LANES), f32),
            pltpu.VMEM((slots * slot_width, hour_count * LANES), bf16),
            pltpu.VMEM((slots * slot_width, hour_count * LANES), bf16),
            pltpu.VMEM((nz, hour_count, tile_count, LANES), f32),
            pltpu.VMEM((plus, hour_count, tile_count, LANES), f32),
            pltpu.VMEM((minus, hour_count, tile_count, LANES), f32),
            dma((2,)),
            dma((2, plus)),
            dma((2, plus)),
            dma((nobs,)),
            dma((nobs,)),
            dma((nobs,)),
            dma((nobs,)),
            dma((nobs,)),
            dma((nobs,)),
            dma((plus, hour_count)),
            dma((plus, hour_count)),
            dma((minus, hour_count)),
            dma((minus, hour_count)),
        ],
        compiler_params=pltpu.CompilerParams(
            collective_id=0, has_side_effects=True, vmem_limit_bytes=40 << 20
        ),
        name="transport",
    )(feet, flux.transpose(1, 0, 2), meta)
    own = lax.dynamic_slice_in_dim(mod[0], lax.rem(me, 2) * 64, 64)
    modeled = own.reshape(block_count, sounding_count, lag_count)[:, :, 0]
    return modeled, grad.transpose(1, 0, 2)


def solution(mesh):
    placed = (
        P(("flux", "obs"), None, None, None, None),
        P(("flux", "obs"), None),
        P(("flux", "obs"), None),
        P(),
        P("flux", None, None),
        P(("flux", "obs"), None),
        P(("flux", "obs"), None),
    )
    return jax.shard_map(
        shards,
        mesh=mesh,
        in_specs=placed,
        out_specs=(P(("flux", "obs"), None), P("flux", None, "obs")),
        check_vma=False,
    )
```

```python
import functools

import jax
import jax.numpy as jnp
from jax import lax
from jax.experimental import pallas as pl
from jax.experimental.pallas import tpu as pltpu
from jax.sharding import PartitionSpec as P

MESH = pl.DeviceIdType.MESH
LANES = 128
ROW = 4
PIECES = ((0, 3), (3, 2))


def kernel(
    nz, nobs, hours, feet, flux, hour_in, row_in, seen_in, var_in, mod, grad,
    held, wide, window, own, metas, pairs, onehot, spread, near, parts, total, high, low,
    mine, down, down_leaf, up, up_leaf,
    local_sem, tree_send, tree_recv, meta_send, meta_recv, feet_send, feet_recv,
    part_send, part_recv, sum_send, sum_recv,
):
    f32, bf16 = jnp.float32, jnp.bfloat16
    chips = nobs // 2
    tiles = flux.shape[1]
    count = nz * tiles
    blocks = feet.shape[0]
    width = 2 * blocks
    slots = chips * width
    depth = nz // 4
    z = lax.axis_index("flux")
    me = lax.axis_index("obs")
    chip, core = me // 2, lax.rem(me, 2)
    y, x = chip // ROW, lax.rem(chip, ROW)

    def level(d):
        return lax.rem(z + d + 2 * nz, nz)

    def target(t):
        c = t // 2
        there = lax.rem(y + c // ROW, chips // ROW) * ROW + lax.rem(x + lax.rem(c, ROW), ROW)
        return there * 2 + lax.rem(core + t, 2)

    def source_chip(c):
        return lax.rem(y + chips // ROW - c // ROW, chips // ROW) * ROW + lax.rem(
            x + ROW - lax.rem(c, ROW), ROW
        )

    def source(t):
        return source_chip(t // 2) * 2 + lax.rem(core + t, 2)

    def remote(src, dst, send, recv, to):
        return pltpu.make_async_remote_copy(
            src_ref=src, dst_ref=dst, send_sem=send, recv_sem=recv,
            device_id=to, device_id_type=MESH,
        )

    def cells(i):
        return feet.at[:, :, :, :, pl.ds(pl.multiple_of(i * LANES, LANES), LANES)]

    def feet_copy(t, i):
        to = target(t)
        return remote(
            cells(to), held.at[i // 2, lax.rem(i, 2)], feet_send.at[t], feet_recv.at[t], (z, to)
        )

    def meta_copy(t, i):
        return remote(own, metas.at[i], meta_send.at[t], meta_recv.at[t], (z, target(t)))

    def part_copy(t, i):
        return remote(parts.at[me], parts.at[i], part_send.at[t], part_recv.at[t], (z, target(t)))

    def tree_copy(kind, s, origin):
        at = window.at[:, pl.ds(pl.multiple_of(origin * tiles, tiles), tiles), :]
        to = level((2, 1, -2, -1)[kind])
        return remote(at, at, tree_send.at[kind, s], tree_recv.at[kind, s], (to, me))

    def tree_start(s):
        tree_copy(0, s, level(-2 * s)).start()
        tree_copy(1, s, level(-2 * s)).start()
        if s < depth - 1:
            tree_copy(2, s, level(2 * s)).start()
        tree_copy(3, s, level(2 * s)).start()

    def tree_step(s):
        tree_copy(0, s - 1, level(-2 * s)).wait_recv()
        tree_copy(2, s - 1, level(2 * s)).wait_recv()
        tree_start(s)

    own_feet = pltpu.make_async_copy(cells(me), held.at[chip, core], local_sem.at[0])
    own_flux = pltpu.make_async_copy(
        flux.at[:, :, pl.ds(pl.multiple_of(me * LANES, LANES), LANES)],
        window.at[:, pl.ds(pl.multiple_of(z * tiles, tiles), tiles), :],
        local_sem.at[1],
    )
    own_flux.start()
    own_feet.start()

    barrier = pltpu.get_barrier_semaphore()
    for d in (1, -1, 2, -2):
        pl.semaphore_signal(barrier, inc=1, device_id=(level(d), me), device_id_type=MESH)

    @pl.loop(1, nobs)
    def _(t):
        pl.semaphore_signal(barrier, inc=1, device_id=(z, target(t)), device_id_type=MESH)

    lane4 = lax.broadcasted_iota(jnp.int32, (4, LANES), 1)
    sub4 = lax.broadcasted_iota(jnp.int32, (4, LANES), 0)

    def expand(values, block_at):
        result = jnp.zeros((4, LANES), f32)
        for b in range(blocks):
            result = jnp.where(block_at == b, values[:, b : b + 1], result)
        return result

    def in_row(values):
        chosen = sub4 == lax.rem(lane4 // 2, 4)
        spread_out = expand(values, lax.rem(lane4 // 8, blocks))
        return jnp.sum(jnp.where(chosen, spread_out, 0.0), axis=0, keepdims=True)

    lag = lax.rem(lane4[0:1], 2).astype(f32)
    own[0:1, :] = in_row(hour_in[...].astype(f32)) + lag
    own[1:2, :] = in_row(seen_in[...])
    own[2:3, :] = in_row(var_in[...])
    own[3:4, :] = jnp.zeros((1, LANES), f32)
    own[4:8, :] = expand(row_in[...], lax.rem(lane4, blocks))
    metas[me] = own[...]
    own_flux.wait()
    pl.semaphore_wait(barrier, nobs + 3)

    tree_start(0)

    @pl.loop(1, nobs)
    def _(t):
        meta_copy(t, me).start()

    @pl.loop(1, nobs)
    def _(t):
        feet_copy(t, me).start()

    if depth > 1:
        tree_step(1)

    @pl.loop(1, nobs)
    def _(t):
        meta_copy(t, source(t)).wait_recv()

    lane = lax.broadcasted_iota(jnp.int32, (8, LANES), 1)
    per_half = nobs // 2
    halves = []
    for half in range(2):
        gathered = jnp.zeros((8, LANES), f32)
        for i in range(per_half):
            gathered = jnp.where(lane // blocks == i, metas[half * per_half + i], gathered)
        halves.append(gathered)

    @pl.loop(0, chips)
    def _(g):
        pairs[g] = jnp.where(lane < 64, metas[2 * g], metas[2 * g + 1])

    for half in range(2):
        upright = halves[half].T
        for k in range(4):
            at = k * slots + half * LANES
            along = upright[:, 4 + k : 5 + k]
            tile_on = lax.broadcasted_iota(jnp.int32, (LANES, count), 1).astype(f32)
            onehot[at : at + LANES, :] = jnp.where(tile_on == along, 1.0, 0.0).astype(bf16)
    if depth > 2:
        tree_step(2)
    for half in range(2):
        for k in range(4):
            at = k * slots + half * LANES
            across = halves[half][4 + k : 5 + k, :]
            tile_at = lax.broadcasted_iota(jnp.int32, (count, LANES), 0).astype(f32)
            spread[:, at : at + LANES] = jnp.where(tile_at == across, 1.0, 0.0).astype(bf16)
    for s in range(3, depth):
        tree_step(s)
    tree_copy(0, depth - 1, level(-2 * depth)).wait_recv()
    for s in range(depth):
        tree_copy(1, s, level(-1 - 2 * s)).wait_recv()
        tree_copy(3, s, level(1 + 2 * s)).wait_recv()

    @pl.loop(0, 4)
    def _(k):
        begin = pl.multiple_of(k * slots, LANES)
        pick = onehot[pl.ds(begin, slots), :]
        for h in range(hours):
            near[h, pl.ds(begin, slots), :] = jnp.dot(
                pick, window[h], preferred_element_type=f32
            ).astype(bf16)

    mask_row = lax.broadcasted_iota(jnp.int32, (hours * width, LANES), 0)
    mask_lane = lax.broadcasted_iota(jnp.int32, (hours * width, LANES), 1)
    same_block = lax.rem(mask_row, width) == mask_lane // 8
    hour_of = (mask_row // width).astype(f32)

    def mask(g):
        return same_block & (hour_of == pairs[g, 0:1, :])

    own_feet.wait()

    @pl.loop(0, chips)
    def _(c):
        @pl.when(c > 0)
        def _():
            feet_copy(2 * c, source(2 * c)).wait_recv()

        feet_copy(2 * c + 1, source(2 * c + 1)).wait_recv()
        g = source_chip(c)
        here = jnp.concatenate(
            [held[g, :, :, k].reshape(LANES, LANES) for k in range(4)], axis=1
        )
        wide[g] = here
        flux_rows = []
        for k in range(4):
            begin = pl.multiple_of(k * slots + g * width, width)
            flux_rows.append(
                jnp.concatenate([near[h, pl.ds(begin, width), :] for h in range(hours)], axis=0)
            )
        products = lax.dot_general(
            jnp.concatenate(flux_rows, axis=1), here,
            (((1,), (1,)), ((), ())), preferred_element_type=f32,
        )
        parts[me, pl.ds(g, 1), :] = jnp.sum(
            jnp.where(mask(g), products, 0.0), axis=0, keepdims=True
        )

    @pl.loop(1, nobs)
    def _(t):
        part_copy(t, me).start()

    @pl.loop(1, nobs)
    def _(t):
        part_copy(t, source(t)).wait_recv()

    summed = parts[0]
    for i in range(1, nobs):
        summed = summed + parts[i]
    even = lax.rem(lax.broadcasted_iota(jnp.int32, (chips, LANES), 1), 2) == 0
    total[...] = summed + jnp.where(
        even, pltpu.roll(summed, LANES - 1, 1), pltpu.roll(summed, 1, 1)
    )
    mod[...] = jnp.broadcast_to(total[pl.ds(chip, 1), :], mod.shape)

    @pl.loop(0, chips)
    def _(g):
        misfit = (total[pl.ds(g, 1), :] - pairs[g, 1:2, :]) / pairs[g, 2:3, :]
        scaled = misfit.astype(bf16).astype(f32)
        coefficient = jnp.where(mask(g), scaled, 0.0).astype(bf16)
        terms = jnp.dot(coefficient, wide[g], preferred_element_type=f32)
        upper = terms.astype(bf16)
        lower = (terms - upper.astype(f32)).astype(bf16)
        for k in range(4):
            begin = pl.multiple_of(k * slots + g * width, width)
            for h in range(hours):
                cut = (slice(h * width, (h + 1) * width), slice(k * LANES, (k + 1) * LANES))
                high[pl.ds(begin, width), h * LANES : (h + 1) * LANES] = upper[cut]
                low[pl.ds(begin, width), h * LANES : (h + 1) * LANES] = lower[cut]

    several = LANES // tiles
    lots = count // LANES

    def gradient_rows(q):
        pick = spread[pl.ds(pl.multiple_of(q * LANES, LANES), LANES), :]
        rows = jnp.dot(pick, high[...], preferred_element_type=f32) + jnp.dot(
            pick, low[...], preferred_element_type=f32
        )
        for i in range(several):
            for h in range(hours):
                mine[q * several + i, h] = rows[
                    i * tiles : (i + 1) * tiles, h * LANES : (h + 1) * LANES
                ]

    top = 2 * depth

    def sum_copy(kind, s, p):
        h = pl.ds(PIECES[p][0], PIECES[p][1])
        if kind == 0:
            src = mine.at[level(-top), h] if s == 0 else down.at[s - 1, h]
            dst, to = down.at[s, h], level(-2)
        elif kind == 1:
            src, dst, to = mine.at[level(1 - top + 2 * s), h], down_leaf.at[s, h], level(-1)
        elif kind == 2:
            src, dst, to = up_leaf.at[s, h], up.at[s, h], level(2)
        else:
            src, dst, to = mine.at[level(top - 1 - 2 * s), h], up_leaf.at[s, h], level(1)
        return remote(src, dst, sum_send.at[kind, s, p], sum_recv.at[kind, s, p], (to, me))

    first = level(top) // several
    gradient_rows(first)
    for p in range(len(PIECES)):
        sum_copy(0, 0, p).start()
    if lots > 1:
        @pl.loop(1, lots)
        def _(j):
            gradient_rows(lax.rem(first + j, lots))

    for p in range(len(PIECES)):
        sum_copy(3, 0, p).start()
        sum_copy(1, 0, p).start()
    for s in range(1, depth):
        for p in range(len(PIECES)):
            h = pl.ds(PIECES[p][0], PIECES[p][1])
            sum_copy(3, s - 1, p).wait_recv()
            add = mine[level(top - 2 * s), h]
            if s > 1:
                sum_copy(2, s - 2, p).wait_recv()
                add = add + up[s - 2, h]
            up_leaf[s - 1, h] += add
            sum_copy(2, s - 1, p).start()
        for p in range(len(PIECES)):
            h = pl.ds(PIECES[p][0], PIECES[p][1])
            sum_copy(1, s - 1, p).wait_recv()
            add = mine[level(2 * s - top), h] + down_leaf[s - 1, h]
            sum_copy(0, s - 1, p).wait_recv()
            down[s - 1, h] += add
            sum_copy(0, s, p).start()
        for p in range(len(PIECES)):
            sum_copy(3, s, p).start()
            sum_copy(1, s, p).start()
    for p in range(len(PIECES)):
        h = pl.ds(PIECES[p][0], PIECES[p][1])
        sum_copy(3, depth - 1, p).wait_recv()
        sum_copy(1, depth - 1, p).wait_recv()
        value = mine[z, h] + up_leaf[depth - 1, h] + down_leaf[depth - 1, h]
        if depth > 1:
            sum_copy(2, depth - 2, p).wait_recv()
            value = value + up[depth - 2, h]
        sum_copy(0, depth - 1, p).wait_recv()
        grad[h] = value + down[depth - 1, h]

    for s in range(depth):
        for kind in range(4):
            if kind == 2 and s == depth - 1:
                continue
            tree_copy(kind, s, z).wait_send()
            for p in range(len(PIECES)):
                sum_copy(kind, s, p).wait_send()

    @pl.loop(1, nobs)
    def _(t):
        meta_copy(t, me).wait_send()
        feet_copy(t, me).wait_send()
        part_copy(t, me).wait_send()


def shards(footprint, obs_hour, tile_list, tile_row, flux, observed, obs_var):
    nobs, nz = lax.axis_size("obs"), lax.axis_size("flux")
    block_count, slot_width, sounding_count, lag_count, cell_count = footprint.shape
    tile_count, hour_count, _ = flux.shape
    me = lax.axis_index("obs")
    f32, bf16 = jnp.float32, jnp.bfloat16
    table_hits = tile_list[..., None] == jnp.arange(tile_row.shape[0], dtype=jnp.int32)
    storage = jnp.sum(jnp.where(table_hits, tile_row, 0), axis=-1).astype(f32)
    chips, count, slots = nobs // 2, nz * tile_count, nobs * block_count
    depth = nz // 4
    chunk = (hour_count, tile_count, LANES)
    dma = pltpu.SemaphoreType.DMA
    vmem = pl.BlockSpec(memory_space=pltpu.VMEM)
    mod, grad = pl.pallas_call(
        functools.partial(kernel, nz, nobs, hour_count),
        out_shape=(
            jax.ShapeDtypeStruct((8, LANES), f32),
            jax.ShapeDtypeStruct(chunk, f32),
        ),
        in_specs=[pl.BlockSpec(memory_space=pl.ANY)] * 2 + [vmem] * 4,
        out_specs=(vmem,) * 2,
        scratch_shapes=[
            pltpu.VMEM((chips, 2) + footprint.shape[:4] + (LANES,), bf16),
            pltpu.VMEM((chips, LANES, slot_width * LANES), bf16),
            pltpu.VMEM((hour_count, count, LANES), bf16),
            pltpu.VMEM((8, LANES), f32),
            pltpu.VMEM((nobs, 8, LANES), f32),
            pltpu.VMEM((chips, 8, LANES), f32),
            pltpu.VMEM((slots * slot_width, count), bf16),
            pltpu.VMEM((count, slots * slot_width), bf16),
            pltpu.VMEM((hour_count, slots * slot_width, LANES), bf16),
            pltpu.VMEM((nobs, chips, LANES), f32),
            pltpu.VMEM((chips, LANES), f32),
            pltpu.VMEM((slots * slot_width, hour_count * LANES), bf16),
            pltpu.VMEM((slots * slot_width, hour_count * LANES), bf16),
            pltpu.VMEM((nz,) + chunk, f32),
            pltpu.VMEM((depth,) + chunk, f32),
            pltpu.VMEM((depth,) + chunk, f32),
            pltpu.VMEM((depth,) + chunk, f32),
            pltpu.VMEM((depth,) + chunk, f32),
            dma((2,)),
            dma((4, depth)),
            dma((4, depth)),
            dma((nobs,)),
            dma((nobs,)),
            dma((nobs,)),
            dma((nobs,)),
            dma((nobs,)),
            dma((nobs,)),
            dma((4, depth, len(PIECES))),
            dma((4, depth, len(PIECES))),
        ],
        compiler_params=pltpu.CompilerParams(
            collective_id=0, has_side_effects=True, vmem_limit_bytes=40 << 20
        ),
        name="transport",
    )(footprint, flux.transpose(1, 0, 2), obs_hour.T, storage.T, observed.T, obs_var.T)
    mine = lax.dynamic_slice_in_dim(mod[0], lax.rem(me, 2) * 64, 64)
    modeled = mine.reshape(block_count, sounding_count, lag_count)[:, :, 0]
    return modeled, grad.transpose(1, 0, 2)


def solution(mesh):
    placed = (
        P(("flux", "obs"), None, None, None, None),
        P(("flux", "obs"), None),
        P(("flux", "obs"), None),
        P(),
        P("flux", None, None),
        P(("flux", "obs"), None),
        P(("flux", "obs"), None),
    )
    return jax.shard_map(
        shards,
        mesh=mesh,
        in_specs=placed,
        out_specs=(P(("flux", "obs"), None), P("flux", None, "obs")),
        check_vma=False,
    )
```

```python
import functools

import jax
import jax.numpy as jnp
from jax import lax
from jax.experimental import pallas as pl
from jax.experimental.pallas import tpu as pltpu
from jax.sharding import PartitionSpec as P

MESH = pl.DeviceIdType.MESH
LANES = 128
ROW = 4
PIECES = ((0, 3), (3, 2))
STRIDE = 7


def kernel(
    nz, nobs, hours, feet, flux, hour_hbm, list_hbm, row_hbm, seen_hbm, var_hbm, mod, grad,
    hour_in, list_in, row_in, seen_in, var_in, held, wide, window, own, metas, pairs, onehot, spread, near, parts, total, high, low,
    mine, down, down_leaf, up, up_leaf,
    local_sem, tree_send, tree_recv, meta_send, meta_recv, feet_send, feet_recv,
    part_send, part_recv, sum_send, sum_recv,
):
    f32, bf16 = jnp.float32, jnp.bfloat16
    chips = nobs // 2
    tiles = flux.shape[1]
    count = nz * tiles
    blocks = feet.shape[0]
    width = 2 * blocks
    slots = chips * width
    depth = nz // 4
    z = lax.axis_index("flux")
    me = lax.axis_index("obs")
    chip, core = me // 2, lax.rem(me, 2)
    y, x = chip // ROW, lax.rem(chip, ROW)

    side = 1 - 2 * core

    def level(d):
        return lax.rem(z + side * d + 2 * nz, nz)

    def target(t):
        c = t // 2
        there = lax.rem(y + c // ROW, chips // ROW) * ROW + lax.rem(x + lax.rem(c, ROW), ROW)
        return there * 2 + lax.rem(core + t, 2)

    def source_chip(c):
        return lax.rem(y + chips // ROW - c // ROW, chips // ROW) * ROW + lax.rem(
            x + ROW - lax.rem(c, ROW), ROW
        )

    def source(t):
        return source_chip(t // 2) * 2 + lax.rem(core + t, 2)

    def remote(src, dst, send, recv, to):
        return pltpu.make_async_remote_copy(
            src_ref=src, dst_ref=dst, send_sem=send, recv_sem=recv,
            device_id=to, device_id_type=MESH,
        )

    def cells(i):
        return feet.at[:, :, :, :, pl.ds(pl.multiple_of(i * LANES, LANES), LANES)]

    def feet_copy(t, i):
        to = target(t)
        return remote(
            cells(to), held.at[i // 2, lax.rem(i, 2)], feet_send.at[t], feet_recv.at[t], (z, to)
        )

    def meta_copy(t, i):
        return remote(own, metas.at[i], meta_send.at[t], meta_recv.at[t], (z, target(t)))

    def part_copy(t, i):
        return remote(parts.at[me], parts.at[i], part_send.at[t], part_recv.at[t], (z, target(t)))

    def tree_copy(kind, s, origin):
        at = window.at[:, pl.ds(pl.multiple_of(origin * tiles, tiles), tiles), :]
        to = level((2, 1, -2, -1)[kind])
        return remote(at, at, tree_send.at[kind, s], tree_recv.at[kind, s], (to, me))

    def tree_start(s):
        tree_copy(0, s, level(-2 * s)).start()
        tree_copy(1, s, level(-2 * s)).start()
        if s < depth - 1:
            tree_copy(2, s, level(2 * s)).start()
        tree_copy(3, s, level(2 * s)).start()

    def tree_step(s):
        tree_copy(0, s - 1, level(-2 * s)).wait_recv()
        tree_copy(2, s - 1, level(2 * s)).wait_recv()
        tree_start(s)

    own_feet = pltpu.make_async_copy(cells(me), held.at[chip, core], local_sem.at[0])
    own_flux = pltpu.make_async_copy(
        flux.at[:, :, pl.ds(pl.multiple_of(me * LANES, LANES), LANES)],
        window.at[:, pl.ds(pl.multiple_of(z * tiles, tiles), tiles), :],
        local_sem.at[1],
    )
    small = [
        pltpu.make_async_copy(src, dst, local_sem.at[2 + i])
        for i, (src, dst) in enumerate(
            [
                (hour_hbm, hour_in),
                (list_hbm, list_in),
                (row_hbm, row_in),
                (seen_hbm, seen_in),
                (var_hbm, var_in),
            ]
        )
    ]
    own_flux.start()
    for copy in small:
        copy.start()
    own_feet.start()

    barrier = pltpu.get_barrier_semaphore()
    for d in (1, -1, 2, -2):
        pl.semaphore_signal(barrier, inc=1, device_id=(level(d), me), device_id_type=MESH)

    @pl.loop(1, nobs)
    def _(t):
        pl.semaphore_signal(barrier, inc=1, device_id=(z, target(t)), device_id_type=MESH)

    lane4 = lax.broadcasted_iota(jnp.int32, (4, LANES), 1)
    sub4 = lax.broadcasted_iota(jnp.int32, (4, LANES), 0)

    for copy in small:
        copy.wait()

    def expand(columns, block_at):
        result = jnp.zeros((4, LANES), f32)
        for b in range(blocks):
            result = jnp.where(block_at == b, columns[b], result)
        return result

    def in_row(values):
        chosen = sub4 == lax.rem(lane4 // 2, 4)
        columns = [values[:, b : b + 1] for b in range(blocks)]
        spread_out = expand(columns, lax.rem(lane4 // 8, blocks))
        return jnp.sum(jnp.where(chosen, spread_out, 0.0), axis=0, keepdims=True)

    lag = lax.rem(lane4[0:1], 2).astype(f32)
    own[0:1, :] = in_row(hour_in[...].astype(f32)) + lag
    own[1:2, :] = in_row(seen_in[...])
    own[2:3, :] = in_row(var_in[...])
    own[3:4, :] = jnp.zeros((1, LANES), f32)
    listed = list_in[...]
    row_of = row_in[...].astype(f32)
    table_at = lax.broadcasted_iota(jnp.int32, (4, row_of.shape[1]), 1)
    own[4:8, :] = expand(
        [
            jnp.sum(
                jnp.where(table_at == listed[:, b : b + 1], row_of, 0.0), axis=1, keepdims=True
            )
            for b in range(blocks)
        ],
        lax.rem(lane4, blocks),
    )
    metas[me] = own[...]
    own_flux.wait()
    pl.semaphore_wait(barrier, nobs + 3)

    tree_start(0)

    @pl.loop(1, nobs)
    def _(t):
        meta_copy(t, me).start()

    @pl.loop(0, nobs - 1)
    def _(i):
        feet_copy(lax.rem(i * STRIDE, nobs - 1) + 1, me).start()

    if depth > 1:
        tree_step(1)

    @pl.loop(1, nobs)
    def _(t):
        meta_copy(t, source(t)).wait_recv()

    lane = lax.broadcasted_iota(jnp.int32, (8, LANES), 1)
    per_half = nobs // 2
    halves = []
    for half in range(2):
        gathered = jnp.zeros((8, LANES), f32)
        for i in range(per_half):
            gathered = jnp.where(lane // blocks == i, metas[half * per_half + i], gathered)
        halves.append(gathered)

    @pl.loop(0, chips)
    def _(g):
        pairs[g] = jnp.where(lane < 64, metas[2 * g], metas[2 * g + 1])

    for half in range(2):
        upright = halves[half].T
        for k in range(4):
            at = k * slots + half * LANES
            along = upright[:, 4 + k : 5 + k]
            tile_on = lax.broadcasted_iota(jnp.int32, (LANES, count), 1).astype(f32)
            onehot[at : at + LANES, :] = jnp.where(tile_on == along, 1.0, 0.0).astype(bf16)
    if depth > 2:
        tree_step(2)
    for half in range(2):
        for k in range(4):
            at = k * slots + half * LANES
            across = halves[half][4 + k : 5 + k, :]
            tile_at = lax.broadcasted_iota(jnp.int32, (count, LANES), 0).astype(f32)
            spread[:, at : at + LANES] = jnp.where(tile_at == across, 1.0, 0.0).astype(bf16)
    for s in range(3, depth):
        tree_step(s)
    tree_copy(0, depth - 1, level(-2 * depth)).wait_recv()
    for s in range(depth):
        tree_copy(1, s, level(-1 - 2 * s)).wait_recv()
        tree_copy(3, s, level(1 + 2 * s)).wait_recv()

    @pl.loop(0, 4)
    def _(k):
        begin = pl.multiple_of(k * slots, LANES)
        pick = onehot[pl.ds(begin, slots), :]
        for h in range(hours):
            near[h, pl.ds(begin, slots), :] = jnp.dot(
                pick, window[h], preferred_element_type=f32
            ).astype(bf16)

    mask_row = lax.broadcasted_iota(jnp.int32, (hours * width, LANES), 0)
    mask_lane = lax.broadcasted_iota(jnp.int32, (hours * width, LANES), 1)
    same_block = lax.rem(mask_row, width) == mask_lane // 8
    hour_of = (mask_row // width).astype(f32)

    def mask(g):
        return same_block & (hour_of == pairs[g, 0:1, :])

    own_feet.wait()

    @pl.loop(0, chips)
    def _(c):
        @pl.when(c > 0)
        def _():
            feet_copy(2 * c, source(2 * c)).wait_recv()

        feet_copy(2 * c + 1, source(2 * c + 1)).wait_recv()
        g = source_chip(c)
        here = jnp.concatenate(
            [held[g, :, :, k].reshape(LANES, LANES) for k in range(4)], axis=1
        )
        wide[g] = here
        flux_rows = []
        for k in range(4):
            begin = pl.multiple_of(k * slots + g * width, width)
            flux_rows.append(
                jnp.concatenate([near[h, pl.ds(begin, width), :] for h in range(hours)], axis=0)
            )
        products = lax.dot_general(
            jnp.concatenate(flux_rows, axis=1), here,
            (((1,), (1,)), ((), ())), preferred_element_type=f32,
        )
        parts[me, pl.ds(g, 1), :] = jnp.sum(
            jnp.where(mask(g), products, 0.0), axis=0, keepdims=True
        )

    @pl.loop(1, nobs)
    def _(t):
        part_copy(t, me).start()

    @pl.loop(1, nobs)
    def _(t):
        part_copy(t, source(t)).wait_recv()

    summed = parts[0]
    for i in range(1, nobs):
        summed = summed + parts[i]
    even = lax.rem(lax.broadcasted_iota(jnp.int32, (chips, LANES), 1), 2) == 0
    total[...] = summed + jnp.where(
        even, pltpu.roll(summed, LANES - 1, 1), pltpu.roll(summed, 1, 1)
    )

    @pl.loop(0, chips)
    def _(g):
        misfit = (total[pl.ds(g, 1), :] - pairs[g, 1:2, :]) / pairs[g, 2:3, :]
        scaled = misfit.astype(bf16).astype(f32)
        coefficient = jnp.where(mask(g), scaled, 0.0).astype(bf16)
        terms = jnp.dot(coefficient, wide[g], preferred_element_type=f32)
        upper = terms.astype(bf16)
        lower = (terms - upper.astype(f32)).astype(bf16)
        for k in range(4):
            begin = pl.multiple_of(k * slots + g * width, width)
            for h in range(hours):
                cut = (slice(h * width, (h + 1) * width), slice(k * LANES, (k + 1) * LANES))
                high[pl.ds(begin, width), h * LANES : (h + 1) * LANES] = upper[cut]
                low[pl.ds(begin, width), h * LANES : (h + 1) * LANES] = lower[cut]

    several = LANES // tiles
    lots = count // LANES

    def gradient_rows(q):
        pick = spread[pl.ds(pl.multiple_of(q * LANES, LANES), LANES), :]
        rows = jnp.dot(pick, high[...], preferred_element_type=f32) + jnp.dot(
            pick, low[...], preferred_element_type=f32
        )
        for i in range(several):
            for h in range(hours):
                mine[q * several + i, h] = rows[
                    i * tiles : (i + 1) * tiles, h * LANES : (h + 1) * LANES
                ]

    top = 2 * depth

    def sum_copy(kind, s, p):
        h = pl.ds(PIECES[p][0], PIECES[p][1])
        if kind == 0:
            src = mine.at[level(-top), h] if s == 0 else down.at[s - 1, h]
            dst, to = down.at[s, h], level(-2)
        elif kind == 1:
            src, dst, to = mine.at[level(1 - top + 2 * s), h], down_leaf.at[s, h], level(-1)
        elif kind == 2:
            src, dst, to = up_leaf.at[s, h], up.at[s, h], level(2)
        else:
            src, dst, to = mine.at[level(top - 1 - 2 * s), h], up_leaf.at[s, h], level(1)
        return remote(src, dst, sum_send.at[kind, s, p], sum_recv.at[kind, s, p], (to, me))

    first = level(top) // several
    gradient_rows(first)
    for p in range(len(PIECES)):
        sum_copy(0, 0, p).start()
    if lots > 1:
        @pl.loop(1, lots)
        def _(j):
            gradient_rows(lax.rem(first + j, lots))

    for p in range(len(PIECES)):
        sum_copy(3, 0, p).start()
        sum_copy(1, 0, p).start()
    here_row = jnp.broadcast_to(total[pl.ds(chip, 1), :], (4, LANES))
    wanted = jnp.where(lane4 // 2 - (lane4 // 8) * 4 == sub4, here_row, 0.0)
    answer = jnp.zeros((4, blocks), f32)
    block_lane = lax.broadcasted_iota(jnp.int32, (4, blocks), 1)
    for b in range(blocks):
        at = (lane4 // 8 == core * blocks + b) & (lax.rem(lane4, 2) == 0)
        picked = jnp.sum(jnp.where(at, wanted, 0.0), axis=1, keepdims=True)
        answer = jnp.where(block_lane == b, picked, answer)
    mod[...] = answer

    for s in range(1, depth):
        for p in range(len(PIECES)):
            h = pl.ds(PIECES[p][0], PIECES[p][1])
            sum_copy(3, s - 1, p).wait_recv()
            add = mine[level(top - 2 * s), h]
            if s > 1:
                sum_copy(2, s - 2, p).wait_recv()
                add = add + up[s - 2, h]
            up_leaf[s - 1, h] += add
            sum_copy(2, s - 1, p).start()
        for p in range(len(PIECES)):
            h = pl.ds(PIECES[p][0], PIECES[p][1])
            sum_copy(1, s - 1, p).wait_recv()
            add = mine[level(2 * s - top), h] + down_leaf[s - 1, h]
            sum_copy(0, s - 1, p).wait_recv()
            down[s - 1, h] += add
            sum_copy(0, s, p).start()
        for p in range(len(PIECES)):
            sum_copy(3, s, p).start()
            sum_copy(1, s, p).start()
    for p in range(len(PIECES)):
        h = pl.ds(PIECES[p][0], PIECES[p][1])
        sum_copy(3, depth - 1, p).wait_recv()
        sum_copy(1, depth - 1, p).wait_recv()
        value = mine[z, h] + up_leaf[depth - 1, h] + down_leaf[depth - 1, h]
        if depth > 1:
            sum_copy(2, depth - 2, p).wait_recv()
            value = value + up[depth - 2, h]
        sum_copy(0, depth - 1, p).wait_recv()
        grad[h] = value + down[depth - 1, h]

    for s in range(depth):
        for kind in range(4):
            if kind == 2 and s == depth - 1:
                continue
            tree_copy(kind, s, z).wait_send()
            for p in range(len(PIECES)):
                sum_copy(kind, s, p).wait_send()

    @pl.loop(1, nobs)
    def _(t):
        meta_copy(t, me).wait_send()
        feet_copy(t, me).wait_send()
        part_copy(t, me).wait_send()


def shards(footprint, obs_hour, tile_list, tile_row, flux, observed, obs_var):
    nobs, nz = lax.axis_size("obs"), lax.axis_size("flux")
    block_count, slot_width, sounding_count, lag_count, cell_count = footprint.shape
    tile_count, hour_count, _ = flux.shape
    f32, bf16 = jnp.float32, jnp.bfloat16
    chips, count, slots = nobs // 2, nz * tile_count, nobs * block_count
    depth = nz // 4
    chunk = (hour_count, tile_count, LANES)
    dma = pltpu.SemaphoreType.DMA
    vmem = pl.BlockSpec(memory_space=pltpu.VMEM)
    mod, grad = pl.pallas_call(
        functools.partial(kernel, nz, nobs, hour_count),
        out_shape=(
            jax.ShapeDtypeStruct((sounding_count, block_count), f32),
            jax.ShapeDtypeStruct(chunk, f32),
        ),
        in_specs=[pl.BlockSpec(memory_space=pltpu.HBM)] * 7,
        out_specs=(vmem,) * 2,
        scratch_shapes=[
            pltpu.VMEM((sounding_count, block_count), jnp.int32),
            pltpu.VMEM((slot_width, block_count), jnp.int32),
            pltpu.VMEM((1, count), jnp.int32),
            pltpu.VMEM((sounding_count, block_count), f32),
            pltpu.VMEM((sounding_count, block_count), f32),
            pltpu.VMEM((chips, 2) + footprint.shape[:4] + (LANES,), bf16),
            pltpu.VMEM((chips, LANES, slot_width * LANES), bf16),
            pltpu.VMEM((hour_count, count, LANES), bf16),
            pltpu.VMEM((8, LANES), f32),
            pltpu.VMEM((nobs, 8, LANES), f32),
            pltpu.VMEM((chips, 8, LANES), f32),
            pltpu.VMEM((slots * slot_width, count), bf16),
            pltpu.VMEM((count, slots * slot_width), bf16),
            pltpu.VMEM((hour_count, slots * slot_width, LANES), bf16),
            pltpu.VMEM((nobs, chips, LANES), f32),
            pltpu.VMEM((chips, LANES), f32),
            pltpu.VMEM((slots * slot_width, hour_count * LANES), bf16),
            pltpu.VMEM((slots * slot_width, hour_count * LANES), bf16),
            pltpu.VMEM((nz,) + chunk, f32),
            pltpu.VMEM((depth,) + chunk, f32),
            pltpu.VMEM((depth,) + chunk, f32),
            pltpu.VMEM((depth,) + chunk, f32),
            pltpu.VMEM((depth,) + chunk, f32),
            dma((7,)),
            dma((4, depth)),
            dma((4, depth)),
            dma((nobs,)),
            dma((nobs,)),
            dma((nobs,)),
            dma((nobs,)),
            dma((nobs,)),
            dma((nobs,)),
            dma((4, depth, len(PIECES))),
            dma((4, depth, len(PIECES))),
        ],
        compiler_params=pltpu.CompilerParams(
            collective_id=0, has_side_effects=True, vmem_limit_bytes=60 << 20
        ),
        name="transport",
    )(
        footprint, flux.transpose(1, 0, 2), obs_hour.T, tile_list.T,
        tile_row.reshape(1, count), observed.T, obs_var.T,
    )
    return mod.T, grad.transpose(1, 0, 2)


def solution(mesh):
    placed = (
        P(("flux", "obs"), None, None, None, None),
        P(("flux", "obs"), None),
        P(("flux", "obs"), None),
        P(),
        P("flux", None, None),
        P(("flux", "obs"), None),
        P(("flux", "obs"), None),
    )
    return jax.shard_map(
        shards,
        mesh=mesh,
        in_specs=placed,
        out_specs=(P(("flux", "obs"), None), P("flux", None, "obs")),
        check_vma=False,
    )
```

```python
import functools

import jax
import jax.numpy as jnp
from jax import lax
from jax.experimental import pallas as pl
from jax.experimental.pallas import tpu as pltpu
from jax.sharding import PartitionSpec as P

MESH = pl.DeviceIdType.MESH
LANES = 128
ROW = 4
PIECES = ((0, 2), (2, 2), (4, 1))
ORDER = (
    4, 23, 18, 16, 1, 26, 5, 8, 15, 17, 21, 25, 13, 19, 11, 14,
    24, 29, 7, 20, 9, 10, 22, 6, 12, 27, 3, 2, 30, 28, 31,
)


def hops(t):
    c = t // 2
    return sum(min(d, ROW - d) for d in (c // ROW, c % ROW))


FAR = tuple(sorted(ORDER, key=hops, reverse=True))


def kernel(
    nz, nobs, hours, feet, flux, hour_hbm, list_hbm, row_hbm, seen_hbm, var_hbm, mod, grad,
    hour_in, list_in, row_in, seen_in, var_in, held, wide, window, own, metas, pairs, onehot, spread, near, parts, total, high, low,
    mine, down, down_leaf, up, up_leaf,
    local_sem, tree_send, tree_recv, meta_send, meta_recv, feet_send, feet_recv,
    part_send, part_recv, sum_send, sum_recv,
):
    f32, bf16 = jnp.float32, jnp.bfloat16
    chips = nobs // 2
    tiles = flux.shape[1]
    count = nz * tiles
    blocks = feet.shape[0]
    width = 2 * blocks
    slots = chips * width
    depth = nz // 4
    z = lax.axis_index("flux")
    me = lax.axis_index("obs")
    chip, core = me // 2, lax.rem(me, 2)
    y, x = chip // ROW, lax.rem(chip, ROW)

    side = 1 - 2 * core

    def level(d):
        return lax.rem(z + side * d + 2 * nz, nz)

    def target(t):
        c = t // 2
        there = lax.rem(y + c // ROW, chips // ROW) * ROW + lax.rem(x + lax.rem(c, ROW), ROW)
        return there * 2 + lax.rem(core + t, 2)

    def source_chip(c):
        return lax.rem(y + chips // ROW - c // ROW, chips // ROW) * ROW + lax.rem(
            x + ROW - lax.rem(c, ROW), ROW
        )

    def source(t):
        return source_chip(t // 2) * 2 + lax.rem(core + t, 2)

    def remote(src, dst, send, recv, to):
        return pltpu.make_async_remote_copy(
            src_ref=src, dst_ref=dst, send_sem=send, recv_sem=recv,
            device_id=to, device_id_type=MESH,
        )

    def cells(i):
        return feet.at[:, :, :, :, pl.ds(pl.multiple_of(i * LANES, LANES), LANES)]

    def feet_copy(t, i):
        to = target(t)
        return remote(
            cells(to), held.at[i // 2, lax.rem(i, 2)], feet_send.at[t], feet_recv.at[t], (z, to)
        )

    def meta_copy(t, i):
        return remote(own, metas.at[i], meta_send.at[t], meta_recv.at[t], (z, target(t)))

    def part_copy(t, i):
        return remote(parts.at[me], parts.at[i], part_send.at[t], part_recv.at[t], (z, target(t)))

    def tree_copy(kind, s, origin):
        at = window.at[:, pl.ds(pl.multiple_of(origin * tiles, tiles), tiles), :]
        to = level((2, 1, -2, -1)[kind])
        return remote(at, at, tree_send.at[kind, s], tree_recv.at[kind, s], (to, me))

    def tree_start(s):
        tree_copy(0, s, level(-2 * s)).start()
        tree_copy(1, s, level(-2 * s)).start()
        if s < depth - 1:
            tree_copy(2, s, level(2 * s)).start()
        tree_copy(3, s, level(2 * s)).start()

    def tree_step(s):
        tree_copy(0, s - 1, level(-2 * s)).wait_recv()
        tree_copy(2, s - 1, level(2 * s)).wait_recv()
        tree_start(s)

    own_feet = pltpu.make_async_copy(cells(me), held.at[chip, core], local_sem.at[0])
    own_flux = pltpu.make_async_copy(
        flux.at[:, :, pl.ds(pl.multiple_of(me * LANES, LANES), LANES)],
        window.at[:, pl.ds(pl.multiple_of(z * tiles, tiles), tiles), :],
        local_sem.at[1],
    )
    small = [
        pltpu.make_async_copy(src, dst, local_sem.at[2 + i])
        for i, (src, dst) in enumerate(
            [
                (hour_hbm, hour_in),
                (list_hbm, list_in),
                (row_hbm, row_in),
                (seen_hbm, seen_in),
                (var_hbm, var_in),
            ]
        )
    ]
    own_flux.start()
    for copy in small:
        copy.start()
    own_feet.start()

    barrier = pltpu.get_barrier_semaphore()
    for d in (2, -2, 1, -1):
        pl.semaphore_signal(barrier, inc=1, device_id=(level(d), me), device_id_type=MESH)

    for t in FAR:
        pl.semaphore_signal(barrier, inc=1, device_id=(z, target(t)), device_id_type=MESH)

    lane4 = lax.broadcasted_iota(jnp.int32, (4, LANES), 1)
    sub4 = lax.broadcasted_iota(jnp.int32, (4, LANES), 0)

    for copy in small:
        copy.wait()

    def expand(columns, block_at):
        result = jnp.zeros((4, LANES), f32)
        for b in range(blocks):
            result = jnp.where(block_at == b, columns[b], result)
        return result

    def in_row(values):
        chosen = sub4 == lax.rem(lane4 // 2, 4)
        columns = [values[:, b : b + 1] for b in range(blocks)]
        spread_out = expand(columns, lax.rem(lane4 // 8, blocks))
        return jnp.sum(jnp.where(chosen, spread_out, 0.0), axis=0, keepdims=True)

    lag = lax.rem(lane4[0:1], 2).astype(f32)
    own[0:1, :] = in_row(hour_in[...].astype(f32)) + lag
    own[1:2, :] = in_row(seen_in[...])
    own[2:3, :] = in_row(var_in[...])
    own[3:4, :] = jnp.zeros((1, LANES), f32)
    listed = list_in[...]
    row_of = row_in[...].astype(f32)
    table_at = lax.broadcasted_iota(jnp.int32, (4, row_of.shape[1]), 1)
    own[4:8, :] = expand(
        [
            jnp.sum(
                jnp.where(table_at == listed[:, b : b + 1], row_of, 0.0), axis=1, keepdims=True
            )
            for b in range(blocks)
        ],
        lax.rem(lane4, blocks),
    )
    metas[me] = own[...]
    own_flux.wait()
    pl.semaphore_wait(barrier, nobs + 3)

    tree_start(0)

    for t in FAR:
        meta_copy(t, me).start()

    for t in ORDER:
        feet_copy(t, me).start()

    if depth > 1:
        tree_step(1)

    @pl.loop(1, nobs)
    def _(t):
        meta_copy(t, source(t)).wait_recv()

    lane = lax.broadcasted_iota(jnp.int32, (8, LANES), 1)
    per_half = nobs // 2
    halves = []
    for half in range(2):
        gathered = jnp.zeros((8, LANES), f32)
        for i in range(per_half):
            gathered = jnp.where(lane // blocks == i, metas[half * per_half + i], gathered)
        halves.append(gathered)

    @pl.loop(0, chips)
    def _(g):
        pairs[g] = jnp.where(lane < 64, metas[2 * g], metas[2 * g + 1])

    for half in range(2):
        upright = halves[half].T
        for k in range(4):
            at = k * slots + half * LANES
            along = upright[:, 4 + k : 5 + k]
            tile_on = lax.broadcasted_iota(jnp.int32, (LANES, count), 1).astype(f32)
            onehot[at : at + LANES, :] = jnp.where(tile_on == along, 1.0, 0.0).astype(bf16)
    if depth > 2:
        tree_step(2)
    for half in range(2):
        for k in range(4):
            at = k * slots + half * LANES
            across = halves[half][4 + k : 5 + k, :]
            tile_at = lax.broadcasted_iota(jnp.int32, (count, LANES), 0).astype(f32)
            spread[:, at : at + LANES] = jnp.where(tile_at == across, 1.0, 0.0).astype(bf16)
    for s in range(3, depth):
        tree_step(s)
    tree_copy(0, depth - 1, level(-2 * depth)).wait_recv()
    for s in range(depth):
        tree_copy(1, s, level(-1 - 2 * s)).wait_recv()
        tree_copy(3, s, level(1 + 2 * s)).wait_recv()

    @pl.loop(0, 4)
    def _(k):
        begin = pl.multiple_of(k * slots, LANES)
        pick = onehot[pl.ds(begin, slots), :]
        for h in range(hours):
            near[h, pl.ds(begin, slots), :] = jnp.dot(
                pick, window[h], preferred_element_type=f32
            ).astype(bf16)

    mask_row = lax.broadcasted_iota(jnp.int32, (hours * width, LANES), 0)
    mask_lane = lax.broadcasted_iota(jnp.int32, (hours * width, LANES), 1)
    same_block = lax.rem(mask_row, width) == mask_lane // 8
    hour_of = (mask_row // width).astype(f32)

    def mask(g):
        return same_block & (hour_of == pairs[g, 0:1, :])

    own_feet.wait()

    @pl.loop(0, chips)
    def _(c):
        @pl.when(c > 0)
        def _():
            feet_copy(2 * c, source(2 * c)).wait_recv()

        feet_copy(2 * c + 1, source(2 * c + 1)).wait_recv()
        g = source_chip(c)
        here = jnp.concatenate(
            [held[g, :, :, k].reshape(LANES, LANES) for k in range(4)], axis=1
        )
        wide[g] = here
        flux_rows = []
        for k in range(4):
            begin = pl.multiple_of(k * slots + g * width, width)
            flux_rows.append(
                jnp.concatenate([near[h, pl.ds(begin, width), :] for h in range(hours)], axis=0)
            )
        products = lax.dot_general(
            jnp.concatenate(flux_rows, axis=1), here,
            (((1,), (1,)), ((), ())), preferred_element_type=f32,
        )
        parts[me, pl.ds(g, 1), :] = jnp.sum(
            jnp.where(mask(g), products, 0.0), axis=0, keepdims=True
        )

    for t in FAR:
        part_copy(t, me).start()

    @pl.loop(1, nobs)
    def _(t):
        part_copy(t, source(t)).wait_recv()

    summed = parts[0]
    for i in range(1, nobs):
        summed = summed + parts[i]
    even = lax.rem(lax.broadcasted_iota(jnp.int32, (chips, LANES), 1), 2) == 0
    total[...] = summed + jnp.where(
        even, pltpu.roll(summed, LANES - 1, 1), pltpu.roll(summed, 1, 1)
    )

    @pl.loop(0, chips, unroll=4)
    def _(g):
        misfit = (total[pl.ds(g, 1), :] - pairs[g, 1:2, :]) / pairs[g, 2:3, :]
        scaled = misfit.astype(bf16).astype(f32)
        coefficient = jnp.where(mask(g), scaled, 0.0).astype(bf16)
        terms = jnp.dot(coefficient, wide[g], preferred_element_type=f32)
        upper = terms.astype(bf16)
        lower = (terms - upper.astype(f32)).astype(bf16)
        for k in range(4):
            begin = pl.multiple_of(k * slots + g * width, width)
            for h in range(hours):
                cut = (slice(h * width, (h + 1) * width), slice(k * LANES, (k + 1) * LANES))
                high[pl.ds(begin, width), h * LANES : (h + 1) * LANES] = upper[cut]
                low[pl.ds(begin, width), h * LANES : (h + 1) * LANES] = lower[cut]

    top = 2 * depth

    def gradient_hours(p):
        begin, many = PIECES[p]
        at = slice(begin * LANES, (begin + many) * LANES)

        @pl.loop(0, count // LANES)
        def _(q):
            pick = spread[pl.ds(pl.multiple_of(q * LANES, LANES), LANES), :]
            rows = jnp.dot(pick, high[:, at], preferred_element_type=f32) + jnp.dot(
                pick, low[:, at], preferred_element_type=f32
            )
            for i in range(LANES // tiles):
                for h in range(many):
                    value = rows[i * tiles : (i + 1) * tiles, h * LANES : (h + 1) * LANES]
                    mine[q * (LANES // tiles) + i, begin + h] = value

    def sum_copy(kind, s, p):
        h = pl.ds(PIECES[p][0], PIECES[p][1])
        if kind == 0:
            src = mine.at[level(-top), h] if s == 0 else down.at[s - 1, h]
            dst, to = down.at[s, h], level(-2)
        elif kind == 1:
            src, dst, to = mine.at[level(1 - top + 2 * s), h], down_leaf.at[s, h], level(-1)
        elif kind == 2:
            src, dst, to = up_leaf.at[s, h], up.at[s, h], level(2)
        else:
            src, dst, to = mine.at[level(top - 1 - 2 * s), h], up_leaf.at[s, h], level(1)
        return remote(src, dst, sum_send.at[kind, s, p], sum_recv.at[kind, s, p], (to, me))

    for p in range(len(PIECES)):
        gradient_hours(p)
        sum_copy(0, 0, p).start()
        sum_copy(3, 0, p).start()
        sum_copy(1, 0, p).start()

    here_row = jnp.broadcast_to(total[pl.ds(chip, 1), :], (4, LANES))
    wanted = jnp.where(lane4 // 2 - (lane4 // 8) * 4 == sub4, here_row, 0.0)
    answer = jnp.zeros((4, blocks), f32)
    block_lane = lax.broadcasted_iota(jnp.int32, (4, blocks), 1)
    for b in range(blocks):
        at = (lane4 // 8 == core * blocks + b) & (lax.rem(lane4, 2) == 0)
        picked = jnp.sum(jnp.where(at, wanted, 0.0), axis=1, keepdims=True)
        answer = jnp.where(block_lane == b, picked, answer)
    mod[...] = answer

    for s in range(1, depth):
        for p in range(len(PIECES)):
            h = pl.ds(PIECES[p][0], PIECES[p][1])
            sum_copy(3, s - 1, p).wait_recv()
            add = mine[level(top - 2 * s), h]
            if s > 1:
                sum_copy(2, s - 2, p).wait_recv()
                add = add + up[s - 2, h]
            up_leaf[s - 1, h] += add
            sum_copy(2, s - 1, p).start()
        for p in range(len(PIECES)):
            h = pl.ds(PIECES[p][0], PIECES[p][1])
            sum_copy(1, s - 1, p).wait_recv()
            add = mine[level(2 * s - top), h] + down_leaf[s - 1, h]
            sum_copy(0, s - 1, p).wait_recv()
            down[s - 1, h] += add
            sum_copy(0, s, p).start()
        for p in range(len(PIECES)):
            sum_copy(3, s, p).start()
            sum_copy(1, s, p).start()
    for p in range(len(PIECES)):
        h = pl.ds(PIECES[p][0], PIECES[p][1])
        sum_copy(3, depth - 1, p).wait_recv()
        sum_copy(1, depth - 1, p).wait_recv()
        value = mine[z, h] + up_leaf[depth - 1, h] + down_leaf[depth - 1, h]
        if depth > 1:
            sum_copy(2, depth - 2, p).wait_recv()
            value = value + up[depth - 2, h]
        sum_copy(0, depth - 1, p).wait_recv()
        grad[h] = value + down[depth - 1, h]

    for s in range(depth):
        for kind in range(4):
            if kind == 2 and s == depth - 1:
                continue
            tree_copy(kind, s, z).wait_send()
            for p in range(len(PIECES)):
                sum_copy(kind, s, p).wait_send()

    @pl.loop(1, nobs)
    def _(t):
        meta_copy(t, me).wait_send()
        feet_copy(t, me).wait_send()
        part_copy(t, me).wait_send()


def shards(footprint, obs_hour, tile_list, tile_row, flux, observed, obs_var):
    nobs, nz = lax.axis_size("obs"), lax.axis_size("flux")
    block_count, slot_width, sounding_count, lag_count, cell_count = footprint.shape
    tile_count, hour_count, _ = flux.shape
    f32, bf16 = jnp.float32, jnp.bfloat16
    chips, count, slots = nobs // 2, nz * tile_count, nobs * block_count
    depth = nz // 4
    chunk = (hour_count, tile_count, LANES)
    dma = pltpu.SemaphoreType.DMA
    vmem = pl.BlockSpec(memory_space=pltpu.VMEM)
    mod, grad = pl.pallas_call(
        functools.partial(kernel, nz, nobs, hour_count),
        out_shape=(
            jax.ShapeDtypeStruct((sounding_count, block_count), f32),
            jax.ShapeDtypeStruct(chunk, f32),
        ),
        in_specs=[pl.BlockSpec(memory_space=pltpu.HBM)] * 7,
        out_specs=(vmem,) * 2,
        scratch_shapes=[
            pltpu.VMEM((sounding_count, block_count), jnp.int32),
            pltpu.VMEM((slot_width, block_count), jnp.int32),
            pltpu.VMEM((1, count), jnp.int32),
            pltpu.VMEM((sounding_count, block_count), f32),
            pltpu.VMEM((sounding_count, block_count), f32),
            pltpu.VMEM((chips, 2) + footprint.shape[:4] + (LANES,), bf16),
            pltpu.VMEM((chips, LANES, slot_width * LANES), bf16),
            pltpu.VMEM((hour_count, count, LANES), bf16),
            pltpu.VMEM((8, LANES), f32),
            pltpu.VMEM((nobs, 8, LANES), f32),
            pltpu.VMEM((chips, 8, LANES), f32),
            pltpu.VMEM((slots * slot_width, count), bf16),
            pltpu.VMEM((count, slots * slot_width), bf16),
            pltpu.VMEM((hour_count, slots * slot_width, LANES), bf16),
            pltpu.VMEM((nobs, chips, LANES), f32),
            pltpu.VMEM((chips, LANES), f32),
            pltpu.VMEM((slots * slot_width, hour_count * LANES), bf16),
            pltpu.VMEM((slots * slot_width, hour_count * LANES), bf16),
            pltpu.VMEM((nz,) + chunk, f32),
            pltpu.VMEM((depth,) + chunk, f32),
            pltpu.VMEM((depth,) + chunk, f32),
            pltpu.VMEM((depth,) + chunk, f32),
            pltpu.VMEM((depth,) + chunk, f32),
            dma((7,)),
            dma((4, depth)),
            dma((4, depth)),
            dma((nobs,)),
            dma((nobs,)),
            dma((nobs,)),
            dma((nobs,)),
            dma((nobs,)),
            dma((nobs,)),
            dma((4, depth, len(PIECES))),
            dma((4, depth, len(PIECES))),
        ],
        compiler_params=pltpu.CompilerParams(
            collective_id=0, has_side_effects=True, vmem_limit_bytes=60 << 20
        ),
        name="transport",
    )(
        footprint, flux.transpose(1, 0, 2), obs_hour.T, tile_list.T,
        tile_row.reshape(1, count), observed.T, obs_var.T,
    )
    return mod.T, grad.transpose(1, 0, 2)


def solution(mesh):
    placed = (
        P(("flux", "obs"), None, None, None, None),
        P(("flux", "obs"), None),
        P(("flux", "obs"), None),
        P(),
        P("flux", None, None),
        P(("flux", "obs"), None),
        P(("flux", "obs"), None),
    )
    return jax.shard_map(
        shards,
        mesh=mesh,
        in_specs=placed,
        out_specs=(P(("flux", "obs"), None), P("flux", None, "obs")),
        check_vma=False,
    )
```

```python
import functools

import jax
import jax.numpy as jnp
from jax import lax
from jax.experimental import pallas as pl
from jax.experimental.pallas import tpu as pltpu
from jax.sharding import PartitionSpec as P

MESH = pl.DeviceIdType.MESH
LANES = 128
ROW = 4
PIECES = ((0, 2), (2, 2), (4, 1))
ORDER = (
    4, 23, 18, 16, 1, 26, 5, 8, 15, 17, 21, 25, 13, 19, 11, 14,
    24, 29, 7, 20, 9, 10, 22, 6, 12, 27, 3, 2, 30, 28, 31,
)


def hops(t):
    c = t // 2
    return sum(min(d, ROW - d) for d in (c // ROW, c % ROW))


FAR = tuple(sorted(ORDER, key=hops, reverse=True))


def kernel(
    nz, nobs, hours, feet, flux, hour_hbm, list_hbm, row_hbm, seen_hbm, var_hbm, mod, grad,
    hour_in, list_in, row_in, seen_in, var_in, held, wide, window, own, metas, pairs, onehot, spread, near, parts, total, high, low,
    mine, down, down_leaf, up, up_leaf,
    local_sem, tree_send, tree_recv, meta_send, meta_recv, feet_send, feet_recv,
    part_send, part_recv, sum_send, sum_recv,
):
    f32, bf16 = jnp.float32, jnp.bfloat16
    chips = nobs // 2
    tiles = flux.shape[1]
    count = nz * tiles
    blocks = feet.shape[0]
    width = 2 * blocks
    slots = chips * width
    depth = nz // 4
    z = lax.axis_index("flux")
    me = lax.axis_index("obs")
    chip, core = me // 2, lax.rem(me, 2)
    y, x = chip // ROW, lax.rem(chip, ROW)

    side = 1 - 2 * core

    def level(d):
        return lax.rem(z + side * d + 2 * nz, nz)

    def target(t):
        c = t // 2
        there = lax.rem(y + c // ROW, chips // ROW) * ROW + lax.rem(x + lax.rem(c, ROW), ROW)
        return there * 2 + lax.rem(core + t, 2)

    def source_chip(c):
        return lax.rem(y + chips // ROW - c // ROW, chips // ROW) * ROW + lax.rem(
            x + ROW - lax.rem(c, ROW), ROW
        )

    def source(t):
        return source_chip(t // 2) * 2 + lax.rem(core + t, 2)

    def remote(src, dst, send, recv, to):
        return pltpu.make_async_remote_copy(
            src_ref=src, dst_ref=dst, send_sem=send, recv_sem=recv,
            device_id=to, device_id_type=MESH,
        )

    def cells(i):
        return feet.at[:, :, :, :, pl.ds(pl.multiple_of(i * LANES, LANES), LANES)]

    def feet_copy(t, i):
        to = target(t)
        return remote(
            cells(to), held.at[i // 2, lax.rem(i, 2)], feet_send.at[t], feet_recv.at[t], (z, to)
        )

    def meta_copy(t, i):
        return remote(own, metas.at[i], meta_send.at[t], meta_recv.at[t], (z, target(t)))

    def part_copy(t, i):
        return remote(parts.at[me], parts.at[i], part_send.at[t], part_recv.at[t], (z, target(t)))

    def tree_copy(kind, s, origin):
        at = window.at[:, pl.ds(pl.multiple_of(origin * tiles, tiles), tiles), :]
        to = level((2, 1, -2, -1)[kind])
        return remote(at, at, tree_send.at[kind, s], tree_recv.at[kind, s], (to, me))

    def tree_start(s):
        tree_copy(0, s, level(-2 * s)).start()
        tree_copy(1, s, level(-2 * s)).start()
        if s < depth - 1:
            tree_copy(2, s, level(2 * s)).start()
        tree_copy(3, s, level(2 * s)).start()

    def tree_step(s):
        tree_copy(0, s - 1, level(-2 * s)).wait_recv()
        tree_copy(2, s - 1, level(2 * s)).wait_recv()
        tree_start(s)

    own_feet = pltpu.make_async_copy(cells(me), held.at[chip, core], local_sem.at[0])
    own_flux = pltpu.make_async_copy(
        flux.at[:, :, pl.ds(pl.multiple_of(me * LANES, LANES), LANES)],
        window.at[:, pl.ds(pl.multiple_of(z * tiles, tiles), tiles), :],
        local_sem.at[1],
    )
    small = [
        pltpu.make_async_copy(src, dst, local_sem.at[2 + i])
        for i, (src, dst) in enumerate(
            [
                (hour_hbm, hour_in),
                (list_hbm, list_in),
                (row_hbm, row_in),
                (seen_hbm, seen_in),
                (var_hbm, var_in),
            ]
        )
    ]
    own_flux.start()
    for copy in small:
        copy.start()
    own_feet.start()

    barrier = pltpu.get_barrier_semaphore()
    for d in (2, -2, 1, -1):
        pl.semaphore_signal(barrier, inc=1, device_id=(level(d), me), device_id_type=MESH)

    for t in FAR:
        pl.semaphore_signal(barrier, inc=1, device_id=(z, target(t)), device_id_type=MESH)

    lane4 = lax.broadcasted_iota(jnp.int32, (4, LANES), 1)
    sub4 = lax.broadcasted_iota(jnp.int32, (4, LANES), 0)

    for copy in small:
        copy.wait()

    def expand(columns, block_at):
        result = jnp.zeros((4, LANES), f32)
        for b in range(blocks):
            result = jnp.where(block_at == b, columns[b], result)
        return result

    def in_row(values):
        chosen = sub4 == lax.rem(lane4 // 2, 4)
        columns = [values[:, b : b + 1] for b in range(blocks)]
        spread_out = expand(columns, lax.rem(lane4 // 8, blocks))
        return jnp.sum(jnp.where(chosen, spread_out, 0.0), axis=0, keepdims=True)

    lag = lax.rem(lane4[0:1], 2).astype(f32)
    own[0:1, :] = in_row(hour_in[...].astype(f32)) + lag
    own[1:2, :] = in_row(seen_in[...])
    own[2:3, :] = in_row(var_in[...])
    own[3:4, :] = jnp.zeros((1, LANES), f32)
    listed = list_in[...]
    row_of = row_in[...].astype(f32)
    table_at = lax.broadcasted_iota(jnp.int32, (4, row_of.shape[1]), 1)
    own[4:8, :] = expand(
        [
            jnp.sum(
                jnp.where(table_at == listed[:, b : b + 1], row_of, 0.0), axis=1, keepdims=True
            )
            for b in range(blocks)
        ],
        lax.rem(lane4, blocks),
    )
    metas[me] = own[...]
    own_flux.wait()
    pl.semaphore_wait(barrier, nobs + 3)

    tree_start(0)

    for t in FAR:
        meta_copy(t, me).start()

    for t in ORDER:
        feet_copy(t, me).start()

    if depth > 1:
        tree_step(1)

    @pl.loop(1, nobs)
    def _(t):
        meta_copy(t, source(t)).wait_recv()

    lane = lax.broadcasted_iota(jnp.int32, (8, LANES), 1)
    per_half = nobs // 2
    halves = []
    for half in range(2):
        gathered = jnp.zeros((8, LANES), f32)
        for i in range(per_half):
            gathered = jnp.where(lane // blocks == i, metas[half * per_half + i], gathered)
        halves.append(gathered)

    @pl.loop(0, chips)
    def _(g):
        pairs[g] = jnp.where(lane < 64, metas[2 * g], metas[2 * g + 1])

    for half in range(2):
        upright = halves[half].T
        for k in range(4):
            at = k * slots + half * LANES
            along = upright[:, 4 + k : 5 + k]
            tile_on = lax.broadcasted_iota(jnp.int32, (LANES, count), 1).astype(f32)
            onehot[at : at + LANES, :] = jnp.where(tile_on == along, 1.0, 0.0).astype(bf16)
    if depth > 2:
        tree_step(2)
    for half in range(2):
        for k in range(4):
            at = k * slots + half * LANES
            across = halves[half][4 + k : 5 + k, :]
            tile_at = lax.broadcasted_iota(jnp.int32, (count, LANES), 0).astype(f32)
            spread[:, at : at + LANES] = jnp.where(tile_at == across, 1.0, 0.0).astype(bf16)
    for s in range(3, depth):
        tree_step(s)
    tree_copy(0, depth - 1, level(-2 * depth)).wait_recv()
    for s in range(depth):
        tree_copy(1, s, level(-1 - 2 * s)).wait_recv()
        tree_copy(3, s, level(1 + 2 * s)).wait_recv()

    @pl.loop(0, 4)
    def _(k):
        begin = pl.multiple_of(k * slots, LANES)
        pick = onehot[pl.ds(begin, slots), :]
        for h in range(hours):
            near[h, pl.ds(begin, slots), :] = jnp.dot(
                pick, window[h], preferred_element_type=f32
            ).astype(bf16)

    mask_row = lax.broadcasted_iota(jnp.int32, (hours * width, LANES), 0)
    mask_lane = lax.broadcasted_iota(jnp.int32, (hours * width, LANES), 1)
    same_block = lax.rem(mask_row, width) == mask_lane // 8
    hour_of = (mask_row // width).astype(f32)

    def mask(g):
        return same_block & (hour_of == pairs[g, 0:1, :])

    own_feet.wait()

    @pl.loop(0, chips)
    def _(c):
        @pl.when(c > 0)
        def _():
            feet_copy(2 * c, source(2 * c)).wait_recv()

        feet_copy(2 * c + 1, source(2 * c + 1)).wait_recv()
        g = source_chip(c)
        here = jnp.concatenate(
            [held[g, :, :, k].reshape(LANES, LANES) for k in range(4)], axis=1
        )
        wide[g] = here
        flux_rows = []
        for k in range(4):
            begin = pl.multiple_of(k * slots + g * width, width)
            flux_rows.append(
                jnp.concatenate([near[h, pl.ds(begin, width), :] for h in range(hours)], axis=0)
            )
        products = lax.dot_general(
            jnp.concatenate(flux_rows, axis=1), here,
            (((1,), (1,)), ((), ())), preferred_element_type=f32,
        )
        parts[me, pl.ds(g, 1), :] = jnp.sum(
            jnp.where(mask(g), products, 0.0), axis=0, keepdims=True
        )

    for t in FAR:
        part_copy(t, me).start()

    @pl.loop(1, nobs)
    def _(t):
        part_copy(t, source(t)).wait_recv()

    summed = parts[0]
    for i in range(1, nobs):
        summed = summed + parts[i]
    even = lax.rem(lax.broadcasted_iota(jnp.int32, (chips, LANES), 1), 2) == 0
    total[...] = summed + jnp.where(
        even, pltpu.roll(summed, LANES - 1, 1), pltpu.roll(summed, 1, 1)
    )

    @pl.loop(0, chips, unroll=4)
    def _(g):
        misfit = (total[pl.ds(g, 1), :] - pairs[g, 1:2, :]) / pairs[g, 2:3, :]
        scaled = misfit.astype(bf16).astype(f32)
        coefficient = jnp.where(mask(g), scaled, 0.0).astype(bf16)
        terms = jnp.dot(coefficient, wide[g], preferred_element_type=f32)
        upper = terms.astype(bf16)
        lower = (terms - upper.astype(f32)).astype(bf16)
        for k in range(4):
            begin = pl.multiple_of(k * slots + g * width, width)
            for h in range(hours):
                cut = (slice(h * width, (h + 1) * width), slice(k * LANES, (k + 1) * LANES))
                high[pl.ds(begin, width), h * LANES : (h + 1) * LANES] = upper[cut]
                low[pl.ds(begin, width), h * LANES : (h + 1) * LANES] = lower[cut]

    top = 2 * depth

    def gradient_hours(p):
        begin, many = PIECES[p]
        at = slice(begin * LANES, (begin + many) * LANES)

        @pl.loop(0, count // LANES)
        def _(q):
            pick = spread[pl.ds(pl.multiple_of(q * LANES, LANES), LANES), :]
            rows = jnp.dot(pick, high[:, at], preferred_element_type=f32) + jnp.dot(
                pick, low[:, at], preferred_element_type=f32
            )
            for i in range(LANES // tiles):
                for h in range(many):
                    value = rows[i * tiles : (i + 1) * tiles, h * LANES : (h + 1) * LANES]
                    mine[q * (LANES // tiles) + i, begin + h] = value

    def sum_copy(kind, s, p):
        h = pl.ds(PIECES[p][0], PIECES[p][1])
        if kind == 0:
            src = mine.at[level(-top), h] if s == 0 else down.at[s - 1, h]
            dst, to = down.at[s, h], level(-2)
        elif kind == 1:
            src, dst, to = mine.at[level(1 - top + 2 * s), h], down_leaf.at[s, h], level(-1)
        elif kind == 2:
            src, dst, to = up_leaf.at[s, h], up.at[s, h], level(2)
        else:
            src, dst, to = mine.at[level(top - 1 - 2 * s), h], up_leaf.at[s, h], level(1)
        return remote(src, dst, sum_send.at[kind, s, p], sum_recv.at[kind, s, p], (to, me))

    for p in range(len(PIECES)):
        gradient_hours(p)
        sum_copy(0, 0, p).start()
        sum_copy(3, 0, p).start()
        sum_copy(1, 0, p).start()

    here_row = jnp.broadcast_to(total[pl.ds(chip, 1), :], (4, LANES))
    wanted = jnp.where(lane4 // 2 - (lane4 // 8) * 4 == sub4, here_row, 0.0)
    answer = jnp.zeros((4, blocks), f32)
    block_lane = lax.broadcasted_iota(jnp.int32, (4, blocks), 1)
    for b in range(blocks):
        at = (lane4 // 8 == core * blocks + b) & (lax.rem(lane4, 2) == 0)
        picked = jnp.sum(jnp.where(at, wanted, 0.0), axis=1, keepdims=True)
        answer = jnp.where(block_lane == b, picked, answer)
    mod[...] = answer

    @pl.loop(1, nobs)
    def _(t):
        meta_copy(t, me).wait_send()
        feet_copy(t, me).wait_send()
        part_copy(t, me).wait_send()

    for kind in range(4):
        for s in range(depth - 1 if kind == 2 else depth):
            tree_copy(kind, s, z).wait_send()

    for s in range(1, depth):
        for p in range(len(PIECES)):
            h = pl.ds(PIECES[p][0], PIECES[p][1])
            sum_copy(3, s - 1, p).wait_recv()
            add = mine[level(top - 2 * s), h]
            if s > 1:
                sum_copy(2, s - 2, p).wait_recv()
                add = add + up[s - 2, h]
            up_leaf[s - 1, h] += add
            sum_copy(2, s - 1, p).start()
        for p in range(len(PIECES)):
            h = pl.ds(PIECES[p][0], PIECES[p][1])
            sum_copy(1, s - 1, p).wait_recv()
            add = mine[level(2 * s - top), h] + down_leaf[s - 1, h]
            sum_copy(0, s - 1, p).wait_recv()
            down[s - 1, h] += add
            sum_copy(0, s, p).start()
        for p in range(len(PIECES)):
            sum_copy(3, s, p).start()
            sum_copy(1, s, p).start()
        for kind in range(4):
            for p in range(len(PIECES)):
                sum_copy(kind, s - 1, p).wait_send()
    for p in range(len(PIECES)):
        h = pl.ds(PIECES[p][0], PIECES[p][1])
        sum_copy(3, depth - 1, p).wait_recv()
        sum_copy(1, depth - 1, p).wait_recv()
        value = mine[z, h] + up_leaf[depth - 1, h] + down_leaf[depth - 1, h]
        if depth > 1:
            sum_copy(2, depth - 2, p).wait_recv()
            value = value + up[depth - 2, h]
        sum_copy(0, depth - 1, p).wait_recv()
        grad[h] = value + down[depth - 1, h]

    for kind in (0, 1, 3):
        for p in range(len(PIECES)):
            sum_copy(kind, depth - 1, p).wait_send()


def shards(footprint, obs_hour, tile_list, tile_row, flux, observed, obs_var):
    nobs, nz = lax.axis_size("obs"), lax.axis_size("flux")
    block_count, slot_width, sounding_count, lag_count, cell_count = footprint.shape
    tile_count, hour_count, _ = flux.shape
    f32, bf16 = jnp.float32, jnp.bfloat16
    chips, count, slots = nobs // 2, nz * tile_count, nobs * block_count
    depth = nz // 4
    chunk = (hour_count, tile_count, LANES)
    dma = pltpu.SemaphoreType.DMA
    vmem = pl.BlockSpec(memory_space=pltpu.VMEM)
    mod, grad = pl.pallas_call(
        functools.partial(kernel, nz, nobs, hour_count),
        out_shape=(
            jax.ShapeDtypeStruct((sounding_count, block_count), f32),
            jax.ShapeDtypeStruct(chunk, f32),
        ),
        in_specs=[pl.BlockSpec(memory_space=pltpu.HBM)] * 7,
        out_specs=(vmem,) * 2,
        scratch_shapes=[
            pltpu.VMEM((sounding_count, block_count), jnp.int32),
            pltpu.VMEM((slot_width, block_count), jnp.int32),
            pltpu.VMEM((1, count), jnp.int32),
            pltpu.VMEM((sounding_count, block_count), f32),
            pltpu.VMEM((sounding_count, block_count), f32),
            pltpu.VMEM((chips, 2) + footprint.shape[:4] + (LANES,), bf16),
            pltpu.VMEM((chips, LANES, slot_width * LANES), bf16),
            pltpu.VMEM((hour_count, count, LANES), bf16),
            pltpu.VMEM((8, LANES), f32),
            pltpu.VMEM((nobs, 8, LANES), f32),
            pltpu.VMEM((chips, 8, LANES), f32),
            pltpu.VMEM((slots * slot_width, count), bf16),
            pltpu.VMEM((count, slots * slot_width), bf16),
            pltpu.VMEM((hour_count, slots * slot_width, LANES), bf16),
            pltpu.VMEM((nobs, chips, LANES), f32),
            pltpu.VMEM((chips, LANES), f32),
            pltpu.VMEM((slots * slot_width, hour_count * LANES), bf16),
            pltpu.VMEM((slots * slot_width, hour_count * LANES), bf16),
            pltpu.VMEM((nz,) + chunk, f32),
            pltpu.VMEM((depth,) + chunk, f32),
            pltpu.VMEM((depth,) + chunk, f32),
            pltpu.VMEM((depth,) + chunk, f32),
            pltpu.VMEM((depth,) + chunk, f32),
            dma((7,)),
            dma((4, depth)),
            dma((4, depth)),
            dma((nobs,)),
            dma((nobs,)),
            dma((nobs,)),
            dma((nobs,)),
            dma((nobs,)),
            dma((nobs,)),
            dma((4, depth, len(PIECES))),
            dma((4, depth, len(PIECES))),
        ],
        compiler_params=pltpu.CompilerParams(
            collective_id=0, has_side_effects=True, vmem_limit_bytes=60 << 20
        ),
        name="transport",
    )(
        footprint, flux.transpose(1, 0, 2), obs_hour.T, tile_list.T,
        tile_row.reshape(1, count), observed.T, obs_var.T,
    )
    return mod.T, grad.transpose(1, 0, 2)


def solution(mesh):
    placed = (
        P(("flux", "obs"), None, None, None, None),
        P(("flux", "obs"), None),
        P(("flux", "obs"), None),
        P(),
        P("flux", None, None),
        P(("flux", "obs"), None),
        P(("flux", "obs"), None),
    )
    return jax.shard_map(
        shards,
        mesh=mesh,
        in_specs=placed,
        out_specs=(P(("flux", "obs"), None), P("flux", None, "obs")),
        check_vma=False,
    )
```

```python
import functools

import jax
import jax.numpy as jnp
from jax import lax
from jax.experimental import pallas as pl
from jax.experimental.pallas import tpu as pltpu
from jax.sharding import PartitionSpec as P

MESH = pl.DeviceIdType.MESH
LANES = 128
ROW = 4
PIECES = ((0, 2), (2, 2), (4, 1))
ORDER = (
    4, 23, 18, 16, 1, 26, 5, 8, 15, 17, 21, 25, 13, 19, 11, 14,
    24, 29, 7, 20, 9, 10, 22, 6, 12, 27, 3, 2, 30, 28, 31,
)


def hops(t):
    c = t // 2
    return sum(min(d, ROW - d) for d in (c // ROW, c % ROW))


ARRIVAL = tuple(
    sorted(range(16), key=lambda c: max(ORDER.index(max(2 * c, 1)), ORDER.index(2 * c + 1)))
)
FAR = tuple(sorted(ORDER, key=hops, reverse=True))


def kernel(
    nz, nobs, hours, feet, flux, hour_hbm, list_hbm, row_hbm, seen_hbm, var_hbm, mod, grad,
    hour_in, list_in, row_in, seen_in, var_in, held, wide, window, own, metas, pairs, onehot, spread, near, parts, total, high, low,
    mine, down, down_leaf, up, up_leaf,
    local_sem, tree_send, tree_recv, meta_send, meta_recv, feet_send, feet_recv,
    part_send, part_recv, sum_send, sum_recv,
):
    f32, bf16 = jnp.float32, jnp.bfloat16
    chips = nobs // 2
    tiles = flux.shape[1]
    count = nz * tiles
    blocks = feet.shape[0]
    width = 2 * blocks
    slots = chips * width
    depth = nz // 4
    z = lax.axis_index("flux")
    me = lax.axis_index("obs")
    chip, core = me // 2, lax.rem(me, 2)
    y, x = chip // ROW, lax.rem(chip, ROW)

    side = 1 - 2 * core

    def level(d):
        return lax.rem(z + side * d + 2 * nz, nz)

    def target(t):
        c = t // 2
        there = lax.rem(y + c // ROW, chips // ROW) * ROW + lax.rem(x + lax.rem(c, ROW), ROW)
        return there * 2 + lax.rem(core + t, 2)

    def source_chip(c):
        return lax.rem(y + chips // ROW - c // ROW, chips // ROW) * ROW + lax.rem(
            x + ROW - lax.rem(c, ROW), ROW
        )

    def source(t):
        return source_chip(t // 2) * 2 + lax.rem(core + t, 2)

    def remote(src, dst, send, recv, to):
        return pltpu.make_async_remote_copy(
            src_ref=src, dst_ref=dst, send_sem=send, recv_sem=recv,
            device_id=to, device_id_type=MESH,
        )

    def cells(i):
        return feet.at[:, :, :, :, pl.ds(pl.multiple_of(i * LANES, LANES), LANES)]

    def feet_copy(t, i):
        to = target(t)
        return remote(
            cells(to), held.at[i // 2, lax.rem(i, 2)], feet_send.at[t], feet_recv.at[t], (z, to)
        )

    def meta_copy(t, i):
        return remote(own, metas.at[i], meta_send.at[t], meta_recv.at[t], (z, target(t)))

    def part_copy(t, i):
        return remote(parts.at[me], parts.at[i], part_send.at[t], part_recv.at[t], (z, target(t)))

    def tree_copy(kind, s, origin):
        at = window.at[:, pl.ds(pl.multiple_of(origin * tiles, tiles), tiles), :]
        to = level((2, 1, -2, -1)[kind])
        return remote(at, at, tree_send.at[kind, s], tree_recv.at[kind, s], (to, me))

    def tree_start(s):
        tree_copy(0, s, level(-2 * s)).start()
        tree_copy(1, s, level(-2 * s)).start()
        if s < depth - 1:
            tree_copy(2, s, level(2 * s)).start()
        tree_copy(3, s, level(2 * s)).start()

    def tree_step(s):
        tree_copy(0, s - 1, level(-2 * s)).wait_recv()
        tree_copy(2, s - 1, level(2 * s)).wait_recv()
        tree_start(s)

    own_feet = pltpu.make_async_copy(cells(me), held.at[chip, core], local_sem.at[0])
    own_flux = pltpu.make_async_copy(
        flux.at[:, :, pl.ds(pl.multiple_of(me * LANES, LANES), LANES)],
        window.at[:, pl.ds(pl.multiple_of(z * tiles, tiles), tiles), :],
        local_sem.at[1],
    )
    small = [
        pltpu.make_async_copy(src, dst, local_sem.at[2 + i])
        for i, (src, dst) in enumerate(
            [
                (hour_hbm, hour_in),
                (list_hbm, list_in),
                (row_hbm, row_in),
                (seen_hbm, seen_in),
                (var_hbm, var_in),
            ]
        )
    ]
    own_flux.start()
    for copy in small:
        copy.start()
    own_feet.start()

    barrier = pltpu.get_barrier_semaphore()
    for d in (2, -2, 1, -1):
        pl.semaphore_signal(barrier, inc=1, device_id=(level(d), me), device_id_type=MESH)

    for t in FAR:
        pl.semaphore_signal(barrier, inc=1, device_id=(z, target(t)), device_id_type=MESH)

    lane4 = lax.broadcasted_iota(jnp.int32, (4, LANES), 1)
    sub4 = lax.broadcasted_iota(jnp.int32, (4, LANES), 0)

    for copy in small:
        copy.wait()

    def expand(columns, block_at):
        result = jnp.zeros((4, LANES), f32)
        for b in range(blocks):
            result = jnp.where(block_at == b, columns[b], result)
        return result

    def in_row(values):
        chosen = sub4 == lax.rem(lane4 // 2, 4)
        columns = [values[:, b : b + 1] for b in range(blocks)]
        spread_out = expand(columns, lax.rem(lane4 // 8, blocks))
        return jnp.sum(jnp.where(chosen, spread_out, 0.0), axis=0, keepdims=True)

    lag = lax.rem(lane4[0:1], 2).astype(f32)
    own[0:1, :] = in_row(hour_in[...].astype(f32)) + lag
    own[1:2, :] = in_row(seen_in[...])
    own[2:3, :] = in_row(var_in[...])
    own[3:4, :] = jnp.zeros((1, LANES), f32)
    listed = list_in[...]
    row_of = row_in[...].astype(f32)
    table_at = lax.broadcasted_iota(jnp.int32, (4, row_of.shape[1]), 1)
    own[4:8, :] = expand(
        [
            jnp.sum(
                jnp.where(table_at == listed[:, b : b + 1], row_of, 0.0), axis=1, keepdims=True
            )
            for b in range(blocks)
        ],
        lax.rem(lane4, blocks),
    )
    metas[me] = own[...]
    own_flux.wait()
    pl.semaphore_wait(barrier, nobs + 3)

    tree_start(0)

    for t in FAR:
        meta_copy(t, me).start()

    for t in ORDER:
        feet_copy(t, me).start()

    if depth > 1:
        tree_step(1)

    @pl.loop(1, nobs)
    def _(t):
        meta_copy(t, source(t)).wait_recv()

    lane = lax.broadcasted_iota(jnp.int32, (8, LANES), 1)
    per_half = nobs // 2
    halves = []
    for half in range(2):
        gathered = jnp.zeros((8, LANES), f32)
        for i in range(per_half):
            gathered = jnp.where(lane // blocks == i, metas[half * per_half + i], gathered)
        halves.append(gathered)

    @pl.loop(0, chips)
    def _(g):
        pairs[g] = jnp.where(lane < 64, metas[2 * g], metas[2 * g + 1])

    for half in range(2):
        upright = halves[half].T
        for k in range(4):
            at = k * slots + half * LANES
            along = upright[:, 4 + k : 5 + k]
            tile_on = lax.broadcasted_iota(jnp.int32, (LANES, count), 1).astype(f32)
            onehot[at : at + LANES, :] = jnp.where(tile_on == along, 1.0, 0.0).astype(bf16)
    if depth > 2:
        tree_step(2)
    for half in range(2):
        for k in range(4):
            at = k * slots + half * LANES
            across = halves[half][4 + k : 5 + k, :]
            tile_at = lax.broadcasted_iota(jnp.int32, (count, LANES), 0).astype(f32)
            spread[:, at : at + LANES] = jnp.where(tile_at == across, 1.0, 0.0).astype(bf16)
    for s in range(3, depth):
        tree_step(s)
    tree_copy(0, depth - 1, level(-2 * depth)).wait_recv()
    for s in range(depth):
        tree_copy(1, s, level(-1 - 2 * s)).wait_recv()
        tree_copy(3, s, level(1 + 2 * s)).wait_recv()

    @pl.loop(0, 4)
    def _(k):
        begin = pl.multiple_of(k * slots, LANES)
        pick = onehot[pl.ds(begin, slots), :]
        for h in range(hours):
            near[h, pl.ds(begin, slots), :] = jnp.dot(
                pick, window[h], preferred_element_type=f32
            ).astype(bf16)

    mask_row = lax.broadcasted_iota(jnp.int32, (hours * width, LANES), 0)
    mask_lane = lax.broadcasted_iota(jnp.int32, (hours * width, LANES), 1)
    same_block = lax.rem(mask_row, width) == mask_lane // 8
    hour_of = (mask_row // width).astype(f32)

    def mask(g):
        return same_block & (hour_of == pairs[g, 0:1, :])

    own_feet.wait()

    for c in ARRIVAL:
        if c > 0:
            feet_copy(2 * c, source(2 * c)).wait_recv()
        feet_copy(2 * c + 1, source(2 * c + 1)).wait_recv()
        g = source_chip(c)
        here = jnp.concatenate(
            [held[g, :, :, k].reshape(LANES, LANES) for k in range(4)], axis=1
        )
        wide[g] = here
        flux_rows = []
        for k in range(4):
            begin = pl.multiple_of(k * slots + g * width, width)
            flux_rows.append(
                jnp.concatenate([near[h, pl.ds(begin, width), :] for h in range(hours)], axis=0)
            )
        products = lax.dot_general(
            jnp.concatenate(flux_rows, axis=1), here,
            (((1,), (1,)), ((), ())), preferred_element_type=f32,
        )
        parts[me, pl.ds(g, 1), :] = jnp.sum(
            jnp.where(mask(g), products, 0.0), axis=0, keepdims=True
        )

    for t in FAR:
        part_copy(t, me).start()

    @pl.loop(1, nobs)
    def _(t):
        part_copy(t, source(t)).wait_recv()

    summed = parts[0]
    for i in range(1, nobs):
        summed = summed + parts[i]
    even = lax.rem(lax.broadcasted_iota(jnp.int32, (chips, LANES), 1), 2) == 0
    total[...] = summed + jnp.where(
        even, pltpu.roll(summed, LANES - 1, 1), pltpu.roll(summed, 1, 1)
    )

    @pl.loop(0, chips, unroll=4)
    def _(g):
        misfit = (total[pl.ds(g, 1), :] - pairs[g, 1:2, :]) / pairs[g, 2:3, :]
        scaled = misfit.astype(bf16).astype(f32)
        coefficient = jnp.where(mask(g), scaled, 0.0).astype(bf16)
        terms = jnp.dot(coefficient, wide[g], preferred_element_type=f32)
        upper = terms.astype(bf16)
        lower = (terms - upper.astype(f32)).astype(bf16)
        for k in range(4):
            begin = pl.multiple_of(k * slots + g * width, width)
            for h in range(hours):
                cut = (slice(h * width, (h + 1) * width), slice(k * LANES, (k + 1) * LANES))
                high[pl.ds(begin, width), h * LANES : (h + 1) * LANES] = upper[cut]
                low[pl.ds(begin, width), h * LANES : (h + 1) * LANES] = lower[cut]

    top = 2 * depth

    def gradient_hours(p):
        begin, many = PIECES[p]
        at = slice(begin * LANES, (begin + many) * LANES)

        @pl.loop(0, count // LANES)
        def _(q):
            pick = spread[pl.ds(pl.multiple_of(q * LANES, LANES), LANES), :]
            rows = jnp.dot(pick, high[:, at], preferred_element_type=f32) + jnp.dot(
                pick, low[:, at], preferred_element_type=f32
            )
            for i in range(LANES // tiles):
                for h in range(many):
                    value = rows[i * tiles : (i + 1) * tiles, h * LANES : (h + 1) * LANES]
                    mine[q * (LANES // tiles) + i, begin + h] = value

    def sum_copy(kind, s, p):
        h = pl.ds(PIECES[p][0], PIECES[p][1])
        if kind == 0:
            src = mine.at[level(-top), h] if s == 0 else down.at[s - 1, h]
            dst, to = down.at[s, h], level(-2)
        elif kind == 1:
            src, dst, to = mine.at[level(1 - top + 2 * s), h], down_leaf.at[s, h], level(-1)
        elif kind == 2:
            src, dst, to = up_leaf.at[s, h], up.at[s, h], level(2)
        else:
            src, dst, to = mine.at[level(top - 1 - 2 * s), h], up_leaf.at[s, h], level(1)
        return remote(src, dst, sum_send.at[kind, s, p], sum_recv.at[kind, s, p], (to, me))

    for p in range(len(PIECES)):
        gradient_hours(p)
        sum_copy(0, 0, p).start()
        sum_copy(3, 0, p).start()
        sum_copy(1, 0, p).start()

    here_row = jnp.broadcast_to(total[pl.ds(chip, 1), :], (4, LANES))
    wanted = jnp.where(lane4 // 2 - (lane4 // 8) * 4 == sub4, here_row, 0.0)
    answer = jnp.zeros((4, blocks), f32)
    block_lane = lax.broadcasted_iota(jnp.int32, (4, blocks), 1)
    for b in range(blocks):
        at = (lane4 // 8 == core * blocks + b) & (lax.rem(lane4, 2) == 0)
        picked = jnp.sum(jnp.where(at, wanted, 0.0), axis=1, keepdims=True)
        answer = jnp.where(block_lane == b, picked, answer)
    mod[...] = answer

    @pl.loop(1, nobs)
    def _(t):
        meta_copy(t, me).wait_send()
        feet_copy(t, me).wait_send()
        part_copy(t, me).wait_send()

    for kind in range(4):
        for s in range(depth - 1 if kind == 2 else depth):
            tree_copy(kind, s, z).wait_send()

    for s in range(1, depth):
        for p in range(len(PIECES)):
            h = pl.ds(PIECES[p][0], PIECES[p][1])
            sum_copy(3, s - 1, p).wait_recv()
            add = mine[level(top - 2 * s), h]
            if s > 1:
                sum_copy(2, s - 2, p).wait_recv()
                add = add + up[s - 2, h]
            up_leaf[s - 1, h] += add
            sum_copy(2, s - 1, p).start()
        for p in range(len(PIECES)):
            h = pl.ds(PIECES[p][0], PIECES[p][1])
            sum_copy(1, s - 1, p).wait_recv()
            add = mine[level(2 * s - top), h] + down_leaf[s - 1, h]
            sum_copy(0, s - 1, p).wait_recv()
            down[s - 1, h] += add
            sum_copy(0, s, p).start()
        for p in range(len(PIECES)):
            sum_copy(3, s, p).start()
            sum_copy(1, s, p).start()
        for kind in range(4):
            for p in range(len(PIECES)):
                sum_copy(kind, s - 1, p).wait_send()
    for p in range(len(PIECES)):
        h = pl.ds(PIECES[p][0], PIECES[p][1])
        sum_copy(3, depth - 1, p).wait_recv()
        sum_copy(1, depth - 1, p).wait_recv()
        value = mine[z, h] + up_leaf[depth - 1, h] + down_leaf[depth - 1, h]
        if depth > 1:
            sum_copy(2, depth - 2, p).wait_recv()
            value = value + up[depth - 2, h]
        sum_copy(0, depth - 1, p).wait_recv()
        grad[h] = value + down[depth - 1, h]

    for kind in (0, 1, 3):
        for p in range(len(PIECES)):
            sum_copy(kind, depth - 1, p).wait_send()


def shards(footprint, obs_hour, tile_list, tile_row, flux, observed, obs_var):
    nobs, nz = lax.axis_size("obs"), lax.axis_size("flux")
    block_count, slot_width, sounding_count, lag_count, cell_count = footprint.shape
    tile_count, hour_count, _ = flux.shape
    f32, bf16 = jnp.float32, jnp.bfloat16
    chips, count, slots = nobs // 2, nz * tile_count, nobs * block_count
    depth = nz // 4
    chunk = (hour_count, tile_count, LANES)
    dma = pltpu.SemaphoreType.DMA
    vmem = pl.BlockSpec(memory_space=pltpu.VMEM)
    mod, grad = pl.pallas_call(
        functools.partial(kernel, nz, nobs, hour_count),
        out_shape=(
            jax.ShapeDtypeStruct((sounding_count, block_count), f32),
            jax.ShapeDtypeStruct(chunk, f32),
        ),
        in_specs=[pl.BlockSpec(memory_space=pltpu.HBM)] * 7,
        out_specs=(vmem,) * 2,
        scratch_shapes=[
            pltpu.VMEM((sounding_count, block_count), jnp.int32),
            pltpu.VMEM((slot_width, block_count), jnp.int32),
            pltpu.VMEM((1, count), jnp.int32),
            pltpu.VMEM((sounding_count, block_count), f32),
            pltpu.VMEM((sounding_count, block_count), f32),
            pltpu.VMEM((chips, 2) + footprint.shape[:4] + (LANES,), bf16),
            pltpu.VMEM((chips, LANES, slot_width * LANES), bf16),
            pltpu.VMEM((hour_count, count, LANES), bf16),
            pltpu.VMEM((8, LANES), f32),
            pltpu.VMEM((nobs, 8, LANES), f32),
            pltpu.VMEM((chips, 8, LANES), f32),
            pltpu.VMEM((slots * slot_width, count), bf16),
            pltpu.VMEM((count, slots * slot_width), bf16),
            pltpu.VMEM((hour_count, slots * slot_width, LANES), bf16),
            pltpu.VMEM((nobs, chips, LANES), f32),
            pltpu.VMEM((chips, LANES), f32),
            pltpu.VMEM((slots * slot_width, hour_count * LANES), bf16),
            pltpu.VMEM((slots * slot_width, hour_count * LANES), bf16),
            pltpu.VMEM((nz,) + chunk, f32),
            pltpu.VMEM((depth,) + chunk, f32),
            pltpu.VMEM((depth,) + chunk, f32),
            pltpu.VMEM((depth,) + chunk, f32),
            pltpu.VMEM((depth,) + chunk, f32),
            dma((7,)),
            dma((4, depth)),
            dma((4, depth)),
            dma((nobs,)),
            dma((nobs,)),
            dma((nobs,)),
            dma((nobs,)),
            dma((nobs,)),
            dma((nobs,)),
            dma((4, depth, len(PIECES))),
            dma((4, depth, len(PIECES))),
        ],
        compiler_params=pltpu.CompilerParams(
            collective_id=0, has_side_effects=True, vmem_limit_bytes=60 << 20
        ),
        name="transport",
    )(
        footprint, flux.transpose(1, 0, 2), obs_hour.T, tile_list.T,
        tile_row.reshape(1, count), observed.T, obs_var.T,
    )
    return mod.T, grad.transpose(1, 0, 2)


def solution(mesh):
    placed = (
        P(("flux", "obs"), None, None, None, None),
        P(("flux", "obs"), None),
        P(("flux", "obs"), None),
        P(),
        P("flux", None, None),
        P(("flux", "obs"), None),
        P(("flux", "obs"), None),
    )
    return jax.shard_map(
        shards,
        mesh=mesh,
        in_specs=placed,
        out_specs=(P(("flux", "obs"), None), P("flux", None, "obs")),
        check_vma=False,
    )
```
